32 devices in a mesh: blk: 8 (over z, y), slab: 4 (over x, core).
Axes of the slice: x: 2, y: 2, z: 4, core: 2. Of those that a mesh axis runs over, the one named last changes fastest.
Arguments:
- orbitals: bfloat16 [192, 8, 8, 128], P('blk', 'slab'), may hold values from -6 to 6
- energies: bfloat16 [192], P('blk'), may hold values from -2 to -0.5
- trial_potential: float32 [8, 8, 8, 128], P('blk', 'slab'), may hold values from -6 to 6
- local_potential: float32 [8, 8, 128], P('slab'), may hold values from 0 to 1
- beta: float32 [64, 128], P('slab'), may hold values from -1.25 to 1.25
- support: int32 [64, 128], P('slab'), may hold values from 0 to 2047, as said below
- slot_atom: int32 [64], P('slab'), may hold values from 0 to 31, as said below
- dcoef: float32 [32], replicated, may hold values from 1.5 to 3
Outputs:
- response: float32 [8, 8, 8, 128], P('blk', 'slab')
The draws below stay inside these ranges and needn't reach their ends.
Inputs may be any that keep to these rules, and one draw needn't show every extreme that they name: `support`: on each slab the 16 slots' supports together list every one of its 2048 cells exactly once. `slot_atom`: atom a belongs to slab a // 8; slab k lists each atom of slab k and each atom of slab (k + 1) modulo the slab count exactly once, in an order drawn from the seed.
All inputs are finite; a program needn't handle non-finite values.
Results may differ from the reference program's by a relative error of at most 0.0003.
Values may be sent and summed in bfloat16 or wider, within the bound.
A program may use at most 64 MiB of HBM per device.

```python
import math
import jax
import jax.numpy as jnp
from jax import lax

ORB = 24
POT_DEV = 1
CZ = 2
GY = 8
GX = 128
A_DEV = 8
ITERS = 3
LOC = 16
SUP = 128
NZ = 8
NATOM = 32
NORB = 192
NPOT = 8
N_BLK = 8
N_SLAB = 4


def draw_support(key, part):
    keys = jax.random.split(key, N_SLAB)

    def one_slab(slab_key):
        return jax.random.permutation(slab_key, CZ * GY * GX)
    orders = jax.vmap(one_slab)(keys)
    return orders.reshape(N_SLAB * LOC, SUP).astype(jnp.int32)


def draw_slot_atom(key, part):
    keys = jax.random.split(key, N_SLAB)

    def one_slab(slab_key, slab):
        first, second, third = jax.random.split(slab_key, 3)
        owned = slab * A_DEV + jax.random.permutation(first, A_DEV)
        above = (slab + 1) % N_SLAB * A_DEV + jax.random.permutation(second, A_DEV)
        listed = jnp.concatenate([owned, above], 0)
        return listed[jax.random.permutation(third, 2 * A_DEV)]
    lists = jax.vmap(one_slab)(keys, jnp.arange(N_SLAB, dtype=jnp.int32))
    return lists.reshape(-1).astype(jnp.int32)


def shard_levels(key, dims, pieces, least, top_value):
    gain, own = 1.0, jax.random.fold_in(key, 6)
    for dim, shards_of in pieces:
        heights = jnp.exp(jax.random.uniform(jax.random.fold_in(own, dim), (shards_of,), jnp.float32, least / len(pieces), top_value / len(pieces)))
        gain = gain * jnp.repeat(heights, dims[dim] // shards_of).reshape([-1 if axis == dim else 1 for axis in range(len(dims))])
    return gain


def centred(rng, shape, width, limit, pieces=(), kind=jnp.bfloat16):
    drawn = width * jax.random.normal(rng, shape, jnp.float32)
    if pieces:
        drawn = drawn * shard_levels(rng, shape, pieces, -0.22, 0.18)
    return jnp.clip(drawn, -limit, limit).astype(kind)


def setup_inputs(seed: int = 0) -> dict:
    arg_keys = jax.random.split(jax.random.key(seed), 9)
    orbitals = centred(arg_keys[0], (NORB, NZ, GY, GX), 1.0, 6.0, ((0, 8), (1, 4)))
    energies = jnp.clip(-2.0 + 1.5 * jax.random.uniform(arg_keys[1], (NORB,), jnp.float32) ** shard_levels(arg_keys[1], (NORB,), ((0, 8),), -0.2, 0.2), -2.0, -0.5).astype(jnp.bfloat16)
    trial_potential = centred(arg_keys[2], (NPOT, NZ, GY, GX), 1.0, 6.0, ((0, 8), (1, 4)), jnp.float32)
    local_potential = jnp.clip(1.0 * jax.random.uniform(arg_keys[3], (NZ, GY, GX), jnp.float32) ** shard_levels(arg_keys[3], (NZ, GY, GX), ((0, 4),), -0.2, 0.2), 0.0, 1.0)
    beta = centred(arg_keys[4], (LOC * N_SLAB, SUP), (1.0 / SUP ** 0.5), 1.25, ((0, 4),), jnp.float32)
    support = draw_support(jax.random.fold_in(arg_keys[8], 71), 0)
    slot_atom = draw_slot_atom(jax.random.fold_in(arg_keys[8], 71), 0)
    dcoef = jnp.clip(jnp.exp(jax.random.uniform(arg_keys[7], (NATOM,), jnp.float32, math.log(1.5), math.log(3.0))), 1.5, 3.0)
    return dict(orbitals=orbitals, energies=energies, trial_potential=trial_potential, local_potential=local_potential, beta=beta, support=support, slot_atom=slot_atom, dcoef=dcoef)


OMEGA = 0.5


def neighbours(field):
    padded = jnp.pad(field, ((0, 0), (1, 1), (0, 0), (0, 0)))
    total = padded[:, 2:] + padded[:, :-2]
    total = total + jnp.roll(field, 1, axis=2) + jnp.roll(field, -1, axis=2)
    total = total + jnp.roll(field, 1, axis=3) + jnp.roll(field, -1, axis=3)
    return total


def reference(orbitals, energies, trial_potential, local_potential, beta, support, slot_atom, dcoef):
    cells = CZ * GY * GX
    slots = N_SLAB * LOC
    base = (jnp.arange(slots, dtype=jnp.int32) // LOC) * cells
    flat_support = (base[:, None] + support).reshape(-1).astype(jnp.int32)
    onehot = (slot_atom[:, None] == jnp.arange(NATOM, dtype=jnp.int32)[None, :]).astype(jnp.float32)

    def nonlocal_term(field):
        count = field.shape[0]
        flat = field.reshape(count, -1)
        picked = flat[:, flat_support].reshape(count, slots, SUP)
        partial_sums = jnp.sum(picked * beta, axis=-1)
        coefs = jnp.dot(partial_sums, onehot, precision=lax.Precision.HIGHEST) * dcoef
        back = jnp.dot(coefs, onehot.T, precision=lax.Precision.HIGHEST)
        values = (back[:, :, None] * beta).reshape(count, -1)
        result = jnp.zeros_like(flat).at[:, flat_support].set(values)
        return result.reshape(field.shape)

    def one_potential(index):
        holder = (index // POT_DEV).astype(jnp.int32)
        prior = ((holder + N_BLK - 1) % N_BLK).astype(jnp.int32)
        psi = jnp.concatenate([lax.dynamic_slice_in_dim(orbitals, holder * ORB, ORB, 0),
                               lax.dynamic_slice_in_dim(orbitals, prior * ORB, ORB, 0)], 0).astype(jnp.float32)
        eps = jnp.concatenate([lax.dynamic_slice_in_dim(energies, holder * ORB, ORB, 0),
                               lax.dynamic_slice_in_dim(energies, prior * ORB, ORB, 0)], 0).astype(jnp.float32)
        potential = lax.dynamic_index_in_dim(trial_potential, index, 0, keepdims=False)
        rhs = -(potential[None] * psi)
        diag = 3.0 + local_potential[None] - eps[:, None, None, None]
        state = rhs / diag
        for step in range(ITERS):
            image = diag * state - 0.5 * neighbours(state) + nonlocal_term(state)
            state = state + OMEGA * (rhs - image) / diag
        return jnp.sum(psi * state, axis=0)

    return lax.map(one_potential, jnp.arange(NPOT, dtype=jnp.int32))
```

```python
import functools

import jax
import jax.numpy as jnp
from jax import lax
from jax.experimental import pallas as pl
from jax.experimental.pallas import tpu as pltpu
from jax.sharding import PartitionSpec as P

ITERS = 3
ROWS = 8
MESH = pl.DeviceIdType.MESH


def nt_dot(a, b):
    return lax.dot_general(a, b, (((1,), (1,)), ((), ())), preferred_element_type=jnp.float32)


def plan(n, tiles):
    order = [n - 1, 1, 0] + list(range(2, n - 1))
    held = [0] * n
    tasks = []
    for i in range(2 * tiles):
        holder = order[i] if i < n else order[1 + (i - n) % (n - 1)]
        tasks.append((i < tiles, i % tiles, holder, held[holder]))
        held[holder] += 1
    return tasks


def lookup(k, table):
    value = jnp.int32(0)
    for i, entry in enumerate(table):
        if entry:
            value = value + jnp.where(k == i, jnp.int32(entry), jnp.int32(0))
    return value


def kernel(
    cfg, orb, eng, slot_atom_in, pot, locp, beta_in, support_in, dcoef_in, out,
    psi_buf, e_own, e_prior, slot_atom, beta, support, dcoef, pack_buf, part, part_buf,
    psi32, psit, x0, gain, quarter, bh, la, lb, acc, ids, onehot,
    psi_send, psi_recv, e_sems, in_sems, pack_send, pack_recv, part_send, part_recv, go,
):
    n, nb, tiles, slots, planes, gy, gx, atoms = cfg
    rows = planes * gy
    nz = n * planes
    d, k = lax.axis_index("blk"), lax.axis_index("slab")
    before = lax.rem(d + nb - 1, nb)
    after = lax.rem(d + 1, nb)
    sibling = k + 1 - 2 * lax.rem(k, 2)
    tasks = plan(n, tiles)
    root = n - 1
    prior_holders = sorted({h for prior, _, h, _ in tasks if prior})
    takes_prior = functools.reduce(jnp.logical_or, [k == h for h in prior_holders])

    loads = [
        pltpu.make_async_copy(src, dst, in_sems.at[i]) for i, (src, dst) in enumerate((
            (support_in, support), (beta_in, beta), (slot_atom_in, slot_atom),
            (dcoef_in, dcoef), (pot.at[0], pack_buf.at[k, 0]), (locp, pack_buf.at[k, 1]),
            (eng, e_own)))]
    for load in loads:
        load.start()
    barrier = pltpu.get_barrier_semaphore()

    @pl.when(takes_prior)
    def _():
        for j in range(n):
            pl.semaphore_signal(
                barrier, inc=1, device_id=(before, lax.rem(k + j, n)), device_id_type=MESH)

    @pl.when(k != root)
    def _():
        pl.semaphore_signal(barrier, inc=1, device_id=(d, root), device_id_type=MESH)
        pl.semaphore_wait(barrier, len(prior_holders))

    @pl.when(k == root)
    def _():
        pl.semaphore_wait(barrier, n - 1 + len(prior_holders))
        for j in range(n - 1):
            pl.semaphore_signal(go, inc=1, device_id=(d, j), device_id_type=MESH)

    def psi_copy(i):
        prior, tile, holder, slot = tasks[i]
        return pltpu.make_async_remote_copy(
            src_ref=orb.at[tile], dst_ref=psi_buf.at[slot, k],
            send_sem=psi_send.at[i], recv_sem=psi_recv.at[slot, k],
            device_id=(after if prior else d, holder), device_id_type=MESH)

    def psi_arrival(slot, j):
        return pltpu.make_async_copy(
            psi_buf.at[slot, j], psi_buf.at[slot, j], psi_recv.at[slot, j])

    def e_copy(i):
        return pltpu.make_async_remote_copy(
            src_ref=eng, dst_ref=e_prior, send_sem=e_sems.at[i],
            recv_sem=e_sems.at[n], device_id=(after, prior_holders[i]), device_id_type=MESH)

    def pack_copy(j, slab, to):
        return pltpu.make_async_remote_copy(
            src_ref=pack_buf.at[slab], dst_ref=pack_buf.at[slab],
            send_sem=pack_send.at[j], recv_sem=pack_recv.at[slab],
            device_id=(d, to), device_id_type=MESH)

    def pack_arrival(slab):
        return pltpu.make_async_copy(
            pack_buf.at[slab], pack_buf.at[slab], pack_recv.at[slab])

    def part_copy(j):
        to = lax.rem(k + j, n)
        return pltpu.make_async_remote_copy(
            src_ref=part.at[to], dst_ref=part_buf.at[j],
            send_sem=part_send.at[j], recv_sem=part_recv.at[j],
            device_id=(d, to), device_id_type=MESH)

    @pl.when(k == 1)
    def _():
        for i in range(len(prior_holders)):
            e_copy(i).start()

    for i in range(tiles):
        psi_copy(i).start()
    for load in loads:
        load.wait()

    sub_rows = lax.broadcasted_iota(jnp.int32, (rows, gx), 0)
    sub_cols = lax.broadcasted_iota(jnp.int32, (gx, gx), 0)
    lefts, rights = [], []
    for s in range(beta.shape[0]):
        cell = support[s:s + 1, :]
        value = beta[s:s + 1, :]
        b1 = value.astype(jnp.bfloat16).astype(jnp.float32)
        b2 = (value - b1).astype(jnp.bfloat16).astype(jnp.float32)
        b3 = value - b1 - b2
        hit = sub_rows == lax.shift_right_logical(cell, 7)
        atom = jnp.full((1, 1), slot_atom[s], jnp.int32).astype(jnp.float32)
        lefts.append(jnp.concatenate(
            [jnp.where(hit, b1, 0.0), jnp.where(hit, b2, 0.0),
             jnp.where(hit, b3, 0.0), jnp.where(hit, atom, 0.0)], axis=0).astype(jnp.bfloat16))
        rights.append(jnp.where(sub_cols == (cell & 127), 1.0, 0.0).astype(jnp.bfloat16))
    cells = nt_dot(jnp.concatenate(lefts, axis=1), jnp.concatenate(rights, axis=1))
    cellwise = cells[:rows] + cells[rows:2 * rows] + cells[2 * rows:3 * rows]
    pack_buf[k, 2] = cellwise.reshape(planes, gy, gx)
    pack_buf[k, 3] = cells[3 * rows:].reshape(planes, gy, gx)

    @pl.when(k != root)
    def _():
        pl.semaphore_wait(go, 1)

    pack_copy(0, k, sibling).start()
    for j in range(1, n // 2):
        pack_copy(j, k, lax.rem(k + 2 * j, n)).start()
    for i in range(tiles, 2 * tiles):
        _, tile, holder, slot = tasks[i]

        @pl.when(k == holder)
        def _():
            pltpu.make_async_copy(
                orb.at[tile], psi_buf.at[slot, k], psi_recv.at[slot, k]).start()

        @pl.when(k != holder)
        def _():
            psi_copy(i).start()

    strength = dcoef[...]
    atom_ids = lax.broadcasted_iota(jnp.int32, (atoms, gx), 0).astype(jnp.float32)
    for j in range(1, n // 2):
        slab = lax.rem(k + 2 * j, n)
        pack_arrival(slab).wait()
        pack_copy(n // 2 + j, slab, sibling).start()
    for j in range(n // 2):
        pack_arrival(lax.rem(sibling + 2 * j, n)).wait()

    for z in range(nz):
        slab, p = z // planes, z % planes
        for y in range(gy):
            at = pack_buf[slab, 3, p, y:y + 1, :]
            onehot[z, :, y * gx:(y + 1) * gx] = jnp.where(atom_ids == at, 1.0, 0.0).astype(jnp.bfloat16)
            ids[z, y] = jnp.broadcast_to(at, (ROWS, gx)).astype(jnp.int32)

    def shared(which, z, y):
        return pack_buf[z // planes, which, z % planes, y:y + 1, :]

    def split(value):
        high = value.astype(jnp.bfloat16).astype(jnp.float32)
        return high, value - high

    def project(z, tiles_of_plane):
        both = jnp.concatenate(
            [jnp.concatenate(split(t), axis=0).astype(jnp.bfloat16) for t in tiles_of_plane], axis=1)
        return nt_dot(both, onehot[z])

    def fold(proj):
        return proj[:ROWS] + proj[ROWS:]

    def coefs_of(proj):
        coefs = proj * strength
        if atoms == gx:
            return coefs, coefs
        return coefs, jnp.concatenate([coefs] * (gx // atoms), axis=1)

    def back(coefs, z):
        return [jnp.take_along_axis(coefs, ids[z, y], axis=1, mode="promise_in_bounds") for y in range(gy)]

    def near(field, z):
        plane = field[z]
        sums = []
        for y in range(gy):
            total = (plane[(y + 1) % gy] + plane[(y - 1) % gy]
                     + pltpu.roll(plane[y], 1, 1) + pltpu.roll(plane[y], gx - 1, 1))
            if z > 0:
                total = total + field[z - 1][y]
            if z < nz - 1:
                total = total + field[z + 1][y]
            sums.append(total)
        return sums

    class Planes:
        def __init__(self, make):
            self.make, self.made = make, {}

        def __getitem__(self, z):
            if z not in self.made:
                self.made[z] = self.make(z)
            return self.made[z]

    arrival_order = [j for j in range(n) if j % 2] + [j for j in range(n) if j % 2 == 0]

    def solve(slot, first):
        held_by = [(prior, tile, h) for prior, tile, h, s in tasks if s == slot]
        tile_of = lookup(k, [next((t for _, t, h in held_by if h == i), 0) for i in range(n)])
        priors = [h for prior, _, h in held_by if prior]
        if not priors:
            held = e_own[...].astype(jnp.float32)
        else:
            is_prior = functools.reduce(jnp.logical_or, [k == h for h in priors])

            @pl.when(is_prior)
            def _():
                e_copy(0).wait_recv()

            @pl.when(jnp.logical_not(is_prior))
            def _():
                e_prior[...] = e_own[...]

            held = e_prior[...].astype(jnp.float32)
        held = held.reshape(1, tiles * ROWS)
        wanted = lax.broadcasted_iota(jnp.int32, (ROWS, tiles * ROWS), 0) + ROWS * tile_of
        mine = wanted == lax.broadcasted_iota(jnp.int32, (ROWS, tiles * ROWS), 1)
        energy = jnp.broadcast_to(
            jnp.sum(jnp.where(mine, held, 0.0), axis=1, keepdims=True), (ROWS, gx))

        damp = jnp.zeros((2 * ROWS, atoms), jnp.float32)
        for z in range(nz):
            scaled = []
            for y in range(gy):
                inv = 1.0 / (3.0 + shared(1, z, y) - energy)
                bv = shared(2, z, y)
                half_inv = 0.5 * bv * inv
                gain[z, y] = -(shared(0, z, y) * inv)
                quarter[z, y] = 0.25 * inv
                bh[z, y] = half_inv
                scaled.append(bv * half_inv)
            damp = damp + project(z, scaled)
        damp = fold(damp)

        proj = jnp.zeros((2 * ROWS, atoms), jnp.float32)
        for j in arrival_order:
            psi_arrival(slot, j).wait()
            psi32[...] = psi_buf[slot, j].astype(jnp.float32).reshape(ROWS * rows, gx)
            for p in range(planes):
                z = j * planes + p
                scaled = []
                for y in range(gy):
                    psi = psi32[pl.ds(p * gy + y, ROWS, stride=rows), :]
                    start = gain[z, y] * psi
                    psit[z, y] = psi
                    x0[z, y] = start
                    scaled.append(start * shared(2, z, y))
                proj = proj + project(z, scaled)
        proj = fold(proj)
        coef, coefs = coefs_of(proj)

        start_planes = Planes(lambda z: [x0[z, y] for y in range(gy)])
        proj = jnp.zeros((2 * ROWS, atoms), jnp.float32)
        for z in range(nz):
            sums, scaled = near(start_planes, z), []
            for y in range(gy):
                value = start_planes[z][y] + quarter[z, y] * sums[y]
                la[z, y] = value
                scaled.append(value * shared(2, z, y))
            proj = proj + project(z, scaled)

        src, dst = la, lb
        for step in range(1, ITERS):
            last = step == ITERS - 1
            next_proj = fold(proj) - damp * coef

            def make(z, src=src, coefs=coefs):
                values = back(coefs, z)
                return [src[z, y] - bh[z, y] * values[y] for y in range(gy)]

            state = Planes(make)
            proj = jnp.zeros((2 * ROWS, atoms), jnp.float32)
            for z in range(nz):
                sums, scaled = near(state, z), []
                for y in range(gy):
                    value = 0.5 * (state[z][y] + x0[z, y]) + quarter[z, y] * sums[y]
                    dst[z, y] = value
                    if not last:
                        scaled.append(value * shared(2, z, y))
                if not last:
                    proj = proj + project(z, scaled)
            coef, coefs = coefs_of(next_proj)
            src, dst = dst, src

        for z in range(nz):
            values = back(coefs, z)
            for y in range(gy):
                term = psit[z, y] * (src[z, y] - bh[z, y] * values[y])
                acc[z, y] = term if first else acc[z, y] + term

    if slots > 1:
        acc[...] = jnp.zeros(acc.shape, jnp.float32)
    for slot in reversed(range(slots)):
        holders = sorted({h for _, _, h, s in tasks if s == slot})
        if len(holders) == n:
            solve(slot, slots == 1)
        else:
            if slots == 1:
                acc[...] = jnp.zeros(acc.shape, jnp.float32)

            @pl.when(functools.reduce(jnp.logical_or, [k == h for h in holders]))
            def _(slot=slot):
                solve(slot, slot == slots - 1)

    sub = lax.broadcasted_iota(jnp.int32, (ROWS, gx), 0)

    def reduce_rows(values):
        shift = 1
        while len(values) > 1:
            odd = (sub & shift) != 0
            merged = []
            for a, b in zip(values[0::2], values[1::2]):
                merged.append(jnp.where(odd, b, a) + pltpu.roll(jnp.where(odd, a, b), shift, 0))
            values, shift = merged, 2 * shift
        return values[0]

    for z in range(nz):
        p = z % planes
        part[z // planes, p * gy:(p + 1) * gy, :] = reduce_rows([acc[z, y] for y in range(gy)])
    for j in range(1, n):
        part_copy(j).start()

    for i in range(2 * tiles):
        if tasks[i][0]:
            psi_copy(i).wait_send()
        else:
            @pl.when(k != tasks[i][2])
            def _():
                psi_copy(i).wait_send()
    for j in range(n):
        if j != n // 2:
            pack_copy(j, k, sibling).wait_send()

    @pl.when(k == 1)
    def _():
        for i in range(len(prior_holders)):
            e_copy(i).wait_send()

    total = part[k]
    for j in range(1, n):
        part_copy(j).wait_recv()
        total = total + part_buf[j]
    out[...] = total.reshape(out.shape)

    for j in range(1, n):
        part_copy(j).wait_send()


def shards(orbitals, energies, trial_potential, local_potential, beta, support, slot_atom, dcoef):
    n, nb = lax.axis_size("slab"), lax.axis_size("blk")
    count, planes, gy, gx = orbitals.shape
    tiles = count // ROWS
    slots = -(-2 * tiles // n)
    atoms = dcoef.shape[0]
    nz, rows = n * planes, planes * gy
    orb = orbitals.reshape(tiles, ROWS, planes, gy, gx)
    f32, bf16 = jnp.float32, jnp.bfloat16
    vmem = pl.BlockSpec(memory_space=pltpu.VMEM)
    hbm = pl.BlockSpec(memory_space=pltpu.HBM)
    dma = pltpu.SemaphoreType.DMA
    field = pltpu.VMEM((nz, gy, ROWS, gx), f32)
    return pl.pallas_call(
        functools.partial(kernel, (n, nb, tiles, slots, planes, gy, gx, atoms)),
        out_shape=jax.ShapeDtypeStruct(trial_potential.shape, f32),
        in_specs=[hbm] * 8,
        out_specs=vmem,
        scratch_shapes=[
            pltpu.VMEM((slots, n, ROWS, planes, gy, gx), bf16),
            pltpu.VMEM(energies.shape, bf16),
            pltpu.VMEM(energies.shape, bf16),
            pltpu.SMEM(slot_atom.shape, jnp.int32),
            pltpu.VMEM(beta.shape, f32),
            pltpu.VMEM(support.shape, jnp.int32),
            pltpu.VMEM((1, atoms), f32),
            pltpu.VMEM((n, 4, planes, gy, gx), f32),
            pltpu.VMEM((n, rows, gx), f32),
            pltpu.VMEM((n, rows, gx), f32),
            pltpu.VMEM((ROWS * rows, gx), f32),
            field, field, field, field, field, field, field, field,
            pltpu.VMEM((nz, gy, ROWS, gx), jnp.int32),
            pltpu.VMEM((nz, atoms, gy * gx), bf16),
            dma((2 * tiles,)), dma((slots, n)), dma((n + 1,)), dma((7,)),
            dma((n,)), dma((n,)), dma((n,)), dma((n,)), pltpu.SemaphoreType.REGULAR,
        ],
        compiler_params=pltpu.CompilerParams(
            collective_id=0, has_side_effects=True, vmem_limit_bytes=32 << 20),
    )(*[pltpu.with_memory_space_constraint(a, pltpu.HBM) for a in (
        orb, energies, slot_atom, trial_potential, local_potential, beta, support,
        dcoef.reshape(1, atoms))])


def solution(mesh):
    placed = (
        P("blk", "slab", None, None),
        P("blk"),
        P("blk", "slab", None, None),
        P("slab", None, None),
        P("slab", None),
        P("slab", None),
        P("slab"),
        P(),
    )
    return jax.shard_map(
        shards, mesh=mesh, in_specs=placed, out_specs=P("blk", "slab", None, None), check_vma=False
    )
```

```python
import functools

import jax
import jax.numpy as jnp
from jax import lax
from jax.experimental import pallas as pl
from jax.experimental.pallas import tpu as pltpu
from jax.sharding import PartitionSpec as P

ITERS = 3
ROWS = 8
MESH = pl.DeviceIdType.MESH


def nt_dot(a, b):
    return lax.dot_general(a, b, (((1,), (1,)), ((), ())), preferred_element_type=jnp.float32)


def plan(n, tiles):
    order = [0, n - 1, 1] + list(range(2, n - 1))
    held = [0] * n
    tasks = []
    for i in range(2 * tiles):
        holder = order[i] if i < n else 1 - (i - n) % 2
        tasks.append((i < tiles, i % tiles, holder, held[holder]))
        held[holder] += 1
    return tasks


def lookup(k, table):
    value = jnp.int32(0)
    for i, entry in enumerate(table):
        if entry:
            value = value + jnp.where(k == i, jnp.int32(entry), jnp.int32(0))
    return value


def kernel(
    cfg, orb, eng, slot_atom_in, pot, locp, beta_in, support_in, dcoef_in, out,
    psi_buf, e_own, e_prior, slot_atom, beta, support, dcoef, pack_buf, part, part_buf,
    psi32, psit, x0, gain, quarter, bh, la, lb, acc, ids, onehot,
    psi_send, psi_recv, e_sems, in_sems, pack_send, pack_recv, part_send, part_recv, go, word,
):
    n, nb, tiles, slots, planes, gy, gx, atoms = cfg
    rows = planes * gy
    nz = n * planes
    d, k = lax.axis_index("blk"), lax.axis_index("slab")
    before = lax.rem(d + nb - 1, nb)
    after = lax.rem(d + 1, nb)
    sibling = k + 1 - 2 * lax.rem(k, 2)
    tasks = plan(n, tiles)
    root, second = n - 1, n - 2
    wraps = d == nb - 1
    prior_holders = sorted({h for prior, _, h, _ in tasks if prior})
    takes_prior = functools.reduce(jnp.logical_or, [k == h for h in prior_holders])

    loads = [
        pltpu.make_async_copy(src, dst, in_sems.at[i]) for i, (src, dst) in enumerate((
            (support_in, support), (beta_in, beta), (slot_atom_in, slot_atom),
            (dcoef_in, dcoef), (pot.at[0], pack_buf.at[k, 0]), (locp, pack_buf.at[k, 1]),
            (eng, e_own)))]
    for load in loads:
        load.start()
    barrier = pltpu.get_barrier_semaphore()

    @pl.when(takes_prior)
    def _():
        for j in range(n - 1):
            pl.semaphore_signal(barrier, inc=1, device_id=(before, j), device_id_type=MESH)

    @pl.when(jnp.logical_and(takes_prior, d == 0))
    def _():
        pl.semaphore_signal(barrier, inc=1, device_id=(before, root), device_id_type=MESH)

    @pl.when(k != root)
    def _():
        pl.semaphore_signal(barrier, inc=1, device_id=(d, root), device_id_type=MESH)
        pl.semaphore_wait(barrier, len(prior_holders))

    @pl.when(k == root)
    def _():
        pl.semaphore_wait(barrier, jnp.where(wraps, n - 1 + len(prior_holders), n - 1))
        for j in reversed(range(n - 1)):
            pl.semaphore_signal(go, inc=1, device_id=(d, j), device_id_type=MESH)

    def psi_copy(i):
        prior, tile, holder, slot = tasks[i]
        return pltpu.make_async_remote_copy(
            src_ref=orb.at[tile], dst_ref=psi_buf.at[slot, k],
            send_sem=psi_send.at[i], recv_sem=psi_recv.at[slot, k],
            device_id=(after if prior else d, holder), device_id_type=MESH)

    def psi_arrival(slot, j):
        return pltpu.make_async_copy(
            psi_buf.at[slot, j], psi_buf.at[slot, j], psi_recv.at[slot, j])

    def e_copy(i):
        return pltpu.make_async_remote_copy(
            src_ref=eng, dst_ref=e_prior, send_sem=e_sems.at[i],
            recv_sem=e_sems.at[n], device_id=(after, prior_holders[i]), device_id_type=MESH)

    def pack_copy(j, slab, to):
        return pltpu.make_async_remote_copy(
            src_ref=pack_buf.at[slab], dst_ref=pack_buf.at[slab],
            send_sem=pack_send.at[j], recv_sem=pack_recv.at[slab],
            device_id=(d, to), device_id_type=MESH)

    def pack_arrival(slab):
        return pltpu.make_async_copy(
            pack_buf.at[slab], pack_buf.at[slab], pack_recv.at[slab])

    def part_copy(j):
        to = lax.rem(k + j, n)
        return pltpu.make_async_remote_copy(
            src_ref=part.at[to], dst_ref=part_buf.at[j],
            send_sem=part_send.at[j], recv_sem=part_recv.at[j],
            device_id=(d, to), device_id_type=MESH)

    @pl.when(k == 1)
    def _():
        for i in range(len(prior_holders)):
            e_copy(i).start()

    @pl.when(wraps)
    def _():
        for i in range(tiles):
            psi_copy(i).start()

    @pl.when(k == second)
    def _():
        pl.semaphore_wait(go, 1)

    @pl.when(jnp.logical_and(k == second, jnp.logical_not(wraps)))
    def _():
        pl.semaphore_signal(word, inc=1, device_id=(d, root), device_id_type=MESH)

    for load in loads:
        load.wait()

    sub_rows = lax.broadcasted_iota(jnp.int32, (rows, gx), 0)
    sub_cols = lax.broadcasted_iota(jnp.int32, (gx, gx), 0)
    lefts, rights = [], []
    for s in range(beta.shape[0]):
        cell = support[s:s + 1, :]
        value = beta[s:s + 1, :]
        b1 = value.astype(jnp.bfloat16).astype(jnp.float32)
        b2 = (value - b1).astype(jnp.bfloat16).astype(jnp.float32)
        b3 = value - b1 - b2
        hit = sub_rows == lax.shift_right_logical(cell, 7)
        atom = jnp.full((1, 1), slot_atom[s], jnp.int32).astype(jnp.float32)
        lefts.append(jnp.concatenate(
            [jnp.where(hit, b1, 0.0), jnp.where(hit, b2, 0.0),
             jnp.where(hit, b3, 0.0), jnp.where(hit, atom, 0.0)], axis=0).astype(jnp.bfloat16))
        rights.append(jnp.where(sub_cols == (cell & 127), 1.0, 0.0).astype(jnp.bfloat16))
    cells = nt_dot(jnp.concatenate(lefts, axis=1), jnp.concatenate(rights, axis=1))
    cellwise = cells[:rows] + cells[rows:2 * rows] + cells[2 * rows:3 * rows]
    pack_buf[k, 2] = cellwise.reshape(planes, gy, gx)
    pack_buf[k, 3] = cells[3 * rows:].reshape(planes, gy, gx)

    @pl.when(k < second)
    def _():
        pl.semaphore_wait(go, 1)

    pack_copy(0, k, sibling).start()
    for j in range(1, n // 2):
        pack_copy(j, k, lax.rem(k + 2 * j, n)).start()
    for i in range(tiles, 2 * tiles):
        _, tile, holder, slot = tasks[i]

        @pl.when(k == holder)
        def _():
            pltpu.make_async_copy(
                orb.at[tile], psi_buf.at[slot, k], psi_recv.at[slot, k]).start()

        @pl.when(k != holder)
        def _():
            psi_copy(i).start()

    @pl.when(jnp.logical_and(k == root, jnp.logical_not(wraps)))
    def _():
        pl.semaphore_wait(word, 1)

    @pl.when(jnp.logical_not(wraps))
    def _():
        for i in range(tiles):
            psi_copy(i).start()

    strength = dcoef[...]
    atom_ids = lax.broadcasted_iota(jnp.int32, (atoms, gx), 0).astype(jnp.float32)
    for j in range(1, n // 2):
        slab = lax.rem(k + 2 * j, n)
        pack_arrival(slab).wait()
        pack_copy(n // 2 + j, slab, sibling).start()
    for j in range(n // 2):
        pack_arrival(lax.rem(sibling + 2 * j, n)).wait()

    for z in range(nz):
        slab, p = z // planes, z % planes
        for y in range(gy):
            at = pack_buf[slab, 3, p, y:y + 1, :]
            onehot[z, :, y * gx:(y + 1) * gx] = jnp.where(atom_ids == at, 1.0, 0.0).astype(jnp.bfloat16)
            ids[z, y] = jnp.broadcast_to(at, (ROWS, gx)).astype(jnp.int32)

    def shared(which, z, y):
        return pack_buf[z // planes, which, z % planes, y:y + 1, :]

    def split(value):
        high = value.astype(jnp.bfloat16).astype(jnp.float32)
        return high, value - high

    def project(z, tiles_of_plane):
        both = jnp.concatenate(
            [jnp.concatenate(split(t), axis=0).astype(jnp.bfloat16) for t in tiles_of_plane], axis=1)
        return nt_dot(both, onehot[z])

    def fold(proj):
        return proj[:ROWS] + proj[ROWS:]

    def coefs_of(proj):
        coefs = proj * strength
        if atoms == gx:
            return coefs, coefs
        return coefs, jnp.concatenate([coefs] * (gx // atoms), axis=1)

    def back(coefs, z):
        return [jnp.take_along_axis(coefs, ids[z, y], axis=1, mode="promise_in_bounds") for y in range(gy)]

    def near(field, z):
        plane = field[z]
        sums = []
        for y in range(gy):
            total = (plane[(y + 1) % gy] + plane[(y - 1) % gy]
                     + pltpu.roll(plane[y], 1, 1) + pltpu.roll(plane[y], gx - 1, 1))
            if z > 0:
                total = total + field[z - 1][y]
            if z < nz - 1:
                total = total + field[z + 1][y]
            sums.append(total)
        return sums

    class Planes:
        def __init__(self, make):
            self.make, self.made = make, {}

        def __getitem__(self, z):
            if z not in self.made:
                self.made[z] = self.make(z)
            return self.made[z]

    arrival_order = [j for j in range(n) if j % 2] + [j for j in range(n) if j % 2 == 0]

    def solve(slot, first):
        held_by = [(prior, tile, h) for prior, tile, h, s in tasks if s == slot]
        tile_of = lookup(k, [next((t for _, t, h in held_by if h == i), 0) for i in range(n)])
        priors = [h for prior, _, h in held_by if prior]
        if not priors:
            held = e_own[...].astype(jnp.float32)
        else:
            is_prior = functools.reduce(jnp.logical_or, [k == h for h in priors])

            @pl.when(is_prior)
            def _():
                e_copy(0).wait_recv()

            @pl.when(jnp.logical_not(is_prior))
            def _():
                e_prior[...] = e_own[...]

            held = e_prior[...].astype(jnp.float32)
        held = held.reshape(1, tiles * ROWS)
        wanted = lax.broadcasted_iota(jnp.int32, (ROWS, tiles * ROWS), 0) + ROWS * tile_of
        mine = wanted == lax.broadcasted_iota(jnp.int32, (ROWS, tiles * ROWS), 1)
        energy = jnp.broadcast_to(
            jnp.sum(jnp.where(mine, held, 0.0), axis=1, keepdims=True), (ROWS, gx))

        damp = jnp.zeros((2 * ROWS, atoms), jnp.float32)
        for z in range(nz):
            scaled = []
            for y in range(gy):
                inv = 1.0 / (3.0 + shared(1, z, y) - energy)
                bv = shared(2, z, y)
                half_inv = 0.5 * bv * inv
                gain[z, y] = -(shared(0, z, y) * inv)
                quarter[z, y] = 0.25 * inv
                bh[z, y] = half_inv
                scaled.append(bv * half_inv)
            damp = damp + project(z, scaled)
        damp = fold(damp)

        proj = jnp.zeros((2 * ROWS, atoms), jnp.float32)
        for j in arrival_order:
            psi_arrival(slot, j).wait()
            psi32[...] = psi_buf[slot, j].astype(jnp.float32).reshape(ROWS * rows, gx)
            for p in range(planes):
                z = j * planes + p
                scaled = []
                for y in range(gy):
                    psi = psi32[pl.ds(p * gy + y, ROWS, stride=rows), :]
                    start = gain[z, y] * psi
                    psit[z, y] = psi
                    x0[z, y] = start
                    scaled.append(start * shared(2, z, y))
                proj = proj + project(z, scaled)
        proj = fold(proj)
        coef, coefs = coefs_of(proj)

        start_planes = Planes(lambda z: [x0[z, y] for y in range(gy)])
        proj = jnp.zeros((2 * ROWS, atoms), jnp.float32)
        for z in range(nz):
            sums, scaled = near(start_planes, z), []
            for y in range(gy):
                value = start_planes[z][y] + quarter[z, y] * sums[y]
                la[z, y] = value
                scaled.append(value * shared(2, z, y))
            proj = proj + project(z, scaled)

        src, dst = la, lb
        for step in range(1, ITERS):
            last = step == ITERS - 1
            next_proj = fold(proj) - damp * coef

            def make(z, src=src, coefs=coefs):
                values = back(coefs, z)
                return [src[z, y] - bh[z, y] * values[y] for y in range(gy)]

            state = Planes(make)
            proj = jnp.zeros((2 * ROWS, atoms), jnp.float32)
            for z in range(nz):
                sums, scaled = near(state, z), []
                for y in range(gy):
                    value = 0.5 * (state[z][y] + x0[z, y]) + quarter[z, y] * sums[y]
                    dst[z, y] = value
                    if not last:
                        scaled.append(value * shared(2, z, y))
                if not last:
                    proj = proj + project(z, scaled)
            coef, coefs = coefs_of(next_proj)
            src, dst = dst, src

        for z in range(nz):
            values = back(coefs, z)
            for y in range(gy):
                term = psit[z, y] * (src[z, y] - bh[z, y] * values[y])
                acc[z, y] = term if first else acc[z, y] + term

    if slots > 1:
        acc[...] = jnp.zeros(acc.shape, jnp.float32)
    for slot in reversed(range(slots)):
        holders = sorted({h for _, _, h, s in tasks if s == slot})
        if len(holders) == n:
            solve(slot, slots == 1)
        else:
            if slots == 1:
                acc[...] = jnp.zeros(acc.shape, jnp.float32)

            @pl.when(functools.reduce(jnp.logical_or, [k == h for h in holders]))
            def _(slot=slot):
                solve(slot, slot == slots - 1)

    sub = lax.broadcasted_iota(jnp.int32, (ROWS, gx), 0)

    def reduce_rows(values):
        shift = 1
        while len(values) > 1:
            odd = (sub & shift) != 0
            merged = []
            for a, b in zip(values[0::2], values[1::2]):
                merged.append(jnp.where(odd, b, a) + pltpu.roll(jnp.where(odd, a, b), shift, 0))
            values, shift = merged, 2 * shift
        return values[0]

    for z in range(nz):
        p = z % planes
        part[z // planes, p * gy:(p + 1) * gy, :] = reduce_rows([acc[z, y] for y in range(gy)])
    for j in reversed(range(1, n)):
        part_copy(j).start()

    for i in range(2 * tiles):
        if tasks[i][0]:
            psi_copy(i).wait_send()
        else:
            @pl.when(k != tasks[i][2])
            def _():
                psi_copy(i).wait_send()
    for j in range(n):
        if j != n // 2:
            pack_copy(j, k, sibling).wait_send()

    @pl.when(k == 1)
    def _():
        for i in range(len(prior_holders)):
            e_copy(i).wait_send()

    total = part[k]
    for j in range(1, n):
        part_copy(j).wait_recv()
        total = total + part_buf[j]
    out[...] = total.reshape(out.shape)

    for j in range(1, n):
        part_copy(j).wait_send()


def shards(orbitals, energies, trial_potential, local_potential, beta, support, slot_atom, dcoef):
    n, nb = lax.axis_size("slab"), lax.axis_size("blk")
    count, planes, gy, gx = orbitals.shape
    tiles = count // ROWS
    slots = -(-2 * tiles // n)
    atoms = dcoef.shape[0]
    nz, rows = n * planes, planes * gy
    orb = orbitals.reshape(tiles, ROWS, planes, gy, gx)
    f32, bf16 = jnp.float32, jnp.bfloat16
    vmem = pl.BlockSpec(memory_space=pltpu.VMEM)
    hbm = pl.BlockSpec(memory_space=pltpu.HBM)
    dma = pltpu.SemaphoreType.DMA
    field = pltpu.VMEM((nz, gy, ROWS, gx), f32)
    return pl.pallas_call(
        functools.partial(kernel, (n, nb, tiles, slots, planes, gy, gx, atoms)),
        out_shape=jax.ShapeDtypeStruct(trial_potential.shape, f32),
        in_specs=[hbm] * 8,
        out_specs=vmem,
        scratch_shapes=[
            pltpu.VMEM((slots, n, ROWS, planes, gy, gx), bf16),
            pltpu.VMEM(energies.shape, bf16),
            pltpu.VMEM(energies.shape, bf16),
            pltpu.SMEM(slot_atom.shape, jnp.int32),
            pltpu.VMEM(beta.shape, f32),
            pltpu.VMEM(support.shape, jnp.int32),
            pltpu.VMEM((1, atoms), f32),
            pltpu.VMEM((n, 4, planes, gy, gx), f32),
            pltpu.VMEM((n, rows, gx), f32),
            pltpu.VMEM((n, rows, gx), f32),
            pltpu.VMEM((ROWS * rows, gx), f32),
            field, field, field, field, field, field, field, field,
            pltpu.VMEM((nz, gy, ROWS, gx), jnp.int32),
            pltpu.VMEM((nz, atoms, gy * gx), bf16),
            dma((2 * tiles,)), dma((slots, n)), dma((n + 1,)), dma((7,)),
            dma((n,)), dma((n,)), dma((n,)), dma((n,)), pltpu.SemaphoreType.REGULAR, pltpu.SemaphoreType.REGULAR,
        ],
        compiler_params=pltpu.CompilerParams(
            collective_id=0, has_side_effects=True, vmem_limit_bytes=32 << 20),
    )(*[pltpu.with_memory_space_constraint(a, pltpu.HBM) for a in (
        orb, energies, slot_atom, trial_potential, local_potential, beta, support,
        dcoef.reshape(1, atoms))])


def solution(mesh):
    placed = (
        P("blk", "slab", None, None),
        P("blk"),
        P("blk", "slab", None, None),
        P("slab", None, None),
        P("slab", None),
        P("slab", None),
        P("slab"),
        P(),
    )
    return jax.shard_map(
        shards, mesh=mesh, in_specs=placed, out_specs=P("blk", "slab", None, None), check_vma=False
    )
```

```python
import functools

import jax
import jax.numpy as jnp
from jax import lax
from jax.experimental import pallas as pl
from jax.experimental.pallas import tpu as pltpu
from jax.sharding import PartitionSpec as P

ITERS = 3
ROWS = 8
MESH = pl.DeviceIdType.MESH


def nt_dot(a, b):
    return lax.dot_general(a, b, (((1,), (1,)), ((), ())), preferred_element_type=jnp.float32)


def pick_lanes(values, lanes):
    return lax.gather(
        values, lanes[..., None],
        lax.GatherDimensionNumbers(
            offset_dims=(), collapsed_slice_dims=(1,), start_index_map=(1,),
            operand_batching_dims=(0,), start_indices_batching_dims=(0,)),
        slice_sizes=(1, 1), mode=lax.GatherScatterMode.PROMISE_IN_BOUNDS)


def plan(n, tiles):
    order = [0, n - 1, 1] + list(range(2, n - 1))
    held = [0] * n
    tasks = []
    for i in range(2 * tiles):
        holder = order[i] if i < n else 1 - (i - n) % 2
        tasks.append((i < tiles, i % tiles, holder, held[holder]))
        held[holder] += 1
    return tasks


def lookup(k, table):
    value = jnp.int32(0)
    for i, entry in enumerate(table):
        if entry:
            value = value + jnp.where(k == i, jnp.int32(entry), jnp.int32(0))
    return value


def kernel(
    cfg, orb, eng, slot_atom_in, pot, locp, beta_in, support_in, dcoef_in, out,
    psi_buf, e_own, e_prior, slot_atom, beta, support, dcoef, pack_buf, part,
    psi32, psit, x0, gain, quarter, bh, la, lb, state, acc, pb, ids, onehot,
    psi_send, psi_recv, e_sems, in_sems, pack_send, pack_recv, part_send, part_recv, go, word,
):
    n, nb, tiles, slots, planes, gy, gx, atoms = cfg
    rows = planes * gy
    nz = n * planes
    d, k = lax.axis_index("blk"), lax.axis_index("slab")
    before = lax.rem(d + nb - 1, nb)
    after = lax.rem(d + 1, nb)
    sibling = k + 1 - 2 * lax.rem(k, 2)
    tasks = plan(n, tiles)
    root, second = n - 1, n - 2
    first_turn = sorted(range(tiles), key=lambda i: tasks[i][2] != root)
    wraps = d == nb - 1
    prior_holders = sorted({h for prior, _, h, _ in tasks if prior})
    takes_prior = functools.reduce(jnp.logical_or, [k == h for h in prior_holders])

    loads = [
        pltpu.make_async_copy(src, dst, in_sems.at[i]) for i, (src, dst) in enumerate((
            (support_in, support), (beta_in, beta), (slot_atom_in, slot_atom),
            (dcoef_in, dcoef), (pot.at[0], pack_buf.at[k, 0]), (locp, pack_buf.at[k, 1]),
            (eng, e_own)))]
    for load in loads:
        load.start()
    barrier = pltpu.get_barrier_semaphore()

    @pl.when(takes_prior)
    def _():
        for j in range(n - 1):
            pl.semaphore_signal(barrier, inc=1, device_id=(before, j), device_id_type=MESH)

    @pl.when(jnp.logical_and(takes_prior, d == 0))
    def _():
        pl.semaphore_signal(barrier, inc=1, device_id=(before, root), device_id_type=MESH)

    @pl.when(k != root)
    def _():
        pl.semaphore_signal(barrier, inc=1, device_id=(d, root), device_id_type=MESH)
        pl.semaphore_wait(barrier, len(prior_holders))

    @pl.when(k == root)
    def _():
        pl.semaphore_wait(barrier, jnp.where(wraps, n - 1 + len(prior_holders), n - 1))
        for j in reversed(range(n - 1)):
            pl.semaphore_signal(go, inc=1, device_id=(d, j), device_id_type=MESH)

    def psi_copy(i):
        prior, tile, holder, slot = tasks[i]
        return pltpu.make_async_remote_copy(
            src_ref=orb.at[tile], dst_ref=psi_buf.at[slot, k],
            send_sem=psi_send.at[i], recv_sem=psi_recv.at[slot, k],
            device_id=(after if prior else d, holder), device_id_type=MESH)

    def psi_arrival(slot, j):
        return pltpu.make_async_copy(
            psi_buf.at[slot, j], psi_buf.at[slot, j], psi_recv.at[slot, j])

    def e_copy(i):
        return pltpu.make_async_remote_copy(
            src_ref=eng, dst_ref=e_prior, send_sem=e_sems.at[i],
            recv_sem=e_sems.at[n], device_id=(after, prior_holders[i]), device_id_type=MESH)

    def pack_copy(j, slab, to):
        return pltpu.make_async_remote_copy(
            src_ref=pack_buf.at[slab], dst_ref=pack_buf.at[slab],
            send_sem=pack_send.at[j], recv_sem=pack_recv.at[slab],
            device_id=(d, to), device_id_type=MESH)

    def pack_arrival(slab):
        return pltpu.make_async_copy(
            pack_buf.at[slab], pack_buf.at[slab], pack_recv.at[slab])

    def part_copy(i):
        to = i + jnp.where(k <= i, 1, 0)
        j = lax.rem(to - k + n, n)
        return pltpu.make_async_remote_copy(
            src_ref=part.at[to], dst_ref=out.at[j],
            send_sem=part_send.at[i], recv_sem=part_recv.at[j],
            device_id=(d, to), device_id_type=MESH)

    def part_arrival(j):
        return pltpu.make_async_copy(part.at[j], out.at[j], part_recv.at[j])

    @pl.when(k == 1)
    def _():
        for i in range(len(prior_holders)):
            e_copy(i).start()

    @pl.when(jnp.logical_and(wraps, k < n // 2))
    def _():
        for i in first_turn:
            psi_copy(i).start()

    @pl.when(jnp.logical_and(wraps, k >= n // 2))
    def _():
        for i in range(tiles):
            psi_copy(i).start()

    @pl.when(k == second)
    def _():
        pl.semaphore_wait(go, 1)

    @pl.when(jnp.logical_and(k == second, jnp.logical_not(wraps)))
    def _():
        pl.semaphore_signal(word, inc=1, device_id=(d, root), device_id_type=MESH)

    for load in loads:
        load.wait()

    sub_rows = lax.broadcasted_iota(jnp.int32, (rows, gx), 0)
    sub_cols = lax.broadcasted_iota(jnp.int32, (gx, gx), 0)
    lefts, rights = [], []
    for s in range(beta.shape[0]):
        cell = support[s:s + 1, :]
        value = beta[s:s + 1, :]
        b1 = value.astype(jnp.bfloat16).astype(jnp.float32)
        b2 = (value - b1).astype(jnp.bfloat16).astype(jnp.float32)
        b3 = value - b1 - b2
        hit = sub_rows == lax.shift_right_logical(cell, 7)
        atom = jnp.full((1, 1), slot_atom[s], jnp.int32).astype(jnp.float32)
        lefts.append(jnp.concatenate(
            [jnp.where(hit, b1, 0.0), jnp.where(hit, b2, 0.0),
             jnp.where(hit, b3, 0.0), jnp.where(hit, atom, 0.0)], axis=0).astype(jnp.bfloat16))
        rights.append(jnp.where(sub_cols == (cell & 127), 1.0, 0.0).astype(jnp.bfloat16))
    cells = nt_dot(jnp.concatenate(lefts, axis=1), jnp.concatenate(rights, axis=1))
    cellwise = cells[:rows] + cells[rows:2 * rows] + cells[2 * rows:3 * rows]
    pack_buf[k, 2] = cellwise.reshape(planes, gy, gx)
    pack_buf[k, 3] = cells[3 * rows:].reshape(planes, gy, gx)

    @pl.when(k < second)
    def _():
        pl.semaphore_wait(go, 1)

    pack_copy(0, k, sibling).start()
    for j in range(1, n // 2):
        pack_copy(j, k, lax.rem(k + 2 * j, n)).start()
    for i in range(tiles, 2 * tiles):
        _, tile, holder, slot = tasks[i]

        @pl.when(k == holder)
        def _():
            pltpu.make_async_copy(
                orb.at[tile], psi_buf.at[slot, k], psi_recv.at[slot, k]).start()

        @pl.when(k != holder)
        def _():
            psi_copy(i).start()

    @pl.when(jnp.logical_and(k == root, jnp.logical_not(wraps)))
    def _():
        pl.semaphore_wait(word, 1)

    @pl.when(jnp.logical_not(wraps))
    def _():
        for i in range(tiles):
            psi_copy(i).start()

    strength = dcoef[...]
    atom_ids = lax.broadcasted_iota(jnp.int32, (atoms, gx), 0).astype(jnp.float32)
    for j in range(1, n // 2):
        slab = lax.rem(k + 2 * j, n)
        pack_arrival(slab).wait()
        pack_copy(n // 2 + j, slab, sibling).start()
    for j in range(n // 2):
        pack_arrival(lax.rem(sibling + 2 * j, n)).wait()

    for z in range(nz):
        slab, p = z // planes, z % planes
        for y in range(gy):
            at = pack_buf[slab, 3, p, y:y + 1, :]
            onehot[z, :, y * gx:(y + 1) * gx] = jnp.where(atom_ids == at, 1.0, 0.0).astype(jnp.bfloat16)
            ids[z, y] = jnp.broadcast_to(at, (ROWS, gx)).astype(jnp.int32)

    def shared(which, z, y):
        return pack_buf[z // planes, which, z % planes, y:y + 1, :]

    def split(value):
        high = value.astype(jnp.bfloat16).astype(jnp.float32)
        return high, value - high

    def project(z, tiles_of_plane):
        both = jnp.concatenate(
            [jnp.concatenate(split(t), axis=0).astype(jnp.bfloat16) for t in tiles_of_plane], axis=1)
        return nt_dot(both, onehot[z])

    def fold(projs):
        total = projs[0] * strength + projs[1] * strength
        return total[:ROWS] + total[ROWS:]

    def no_projs():
        return [jnp.zeros((2 * ROWS, atoms), jnp.float32) for _ in range(2)]

    def coefs_of(coefs):
        if atoms == gx:
            return coefs, coefs
        return coefs, jnp.concatenate([coefs, jnp.zeros((ROWS, gx - atoms), jnp.float32)], axis=1)

    def back(coefs, z):
        return [pick_lanes(coefs, ids[z, y]) for y in range(gy)]

    def beside(plane, y):
        return (plane[(y + 1) % gy] + plane[(y - 1) % gy]
                + pltpu.roll(plane[y], 1, 1) + pltpu.roll(plane[y], gx - 1, 1))

    sub = lax.broadcasted_iota(jnp.int32, (ROWS, gx), 0)

    def reduce_rows(values):
        shift = 1
        while len(values) > 1:
            odd = (sub & shift) != 0
            merged = []
            for a, b in zip(values[0::2], values[1::2]):
                merged.append(jnp.where(odd, b, a) + pltpu.roll(jnp.where(odd, a, b), shift, 0))
            values, shift = merged, 2 * shift
        return values[0]

    arrival_order = [j + 1 - 2 * (j % 2) for j in range(n)]

    streams = len({h for _, _, h, s in tasks if s == 0}) == n

    def solve(slot, first):
        held_by = [(prior, tile, h) for prior, tile, h, s in tasks if s == slot]
        tile_of = lookup(k, [next((t for _, t, h in held_by if h == i), 0) for i in range(n)])
        priors = [h for prior, _, h in held_by if prior]
        if not priors:
            held = e_own[...].astype(jnp.float32)
        else:
            is_prior = functools.reduce(jnp.logical_or, [k == h for h in priors])

            @pl.when(is_prior)
            def _():
                e_copy(0).wait_recv()

            @pl.when(jnp.logical_not(is_prior))
            def _():
                e_prior[...] = e_own[...]

            held = e_prior[...].astype(jnp.float32)
        held = held.reshape(1, tiles * ROWS)
        wanted = lax.broadcasted_iota(jnp.int32, (ROWS, tiles * ROWS), 0) + ROWS * tile_of
        mine = wanted == lax.broadcasted_iota(jnp.int32, (ROWS, tiles * ROWS), 1)
        energy = jnp.broadcast_to(
            jnp.sum(jnp.where(mine, held, 0.0), axis=1, keepdims=True), (ROWS, gx))

        damps = no_projs()
        for z in range(nz):
            scaled = []
            for y in range(gy):
                inv = 1.0 / (3.0 + shared(1, z, y) - energy)
                bv = shared(2, z, y)
                half_inv = 0.5 * bv * inv
                gain[z, y] = -(shared(0, z, y) * inv)
                quarter[z, y] = 0.25 * inv
                bh[z, y] = half_inv
                scaled.append(bv * half_inv)
            damps[z % 2] = damps[z % 2] + project(z, scaled)
        damp = fold(damps)

        projs = no_projs()
        for j in arrival_order:
            psi_arrival(slot, j).wait()
            psi32[...] = psi_buf[slot, j].astype(jnp.float32).reshape(ROWS * rows, gx)
            zs = range(j * planes, (j + 1) * planes)
            field = {}
            for z in zs:
                scaled, field[z] = [], []
                for y in range(gy):
                    psi = psi32[pl.ds(z % planes * gy + y, ROWS, stride=rows), :]
                    start = gain[z, y] * psi
                    psit[z, y] = psi
                    pb[z, y] = psi * bh[z, y]
                    x0[z, y] = start
                    field[z].append(start)
                    scaled.append(start * shared(2, z, y))
                projs[z % 2] = projs[z % 2] + project(z, scaled)
            for z in zs:
                for y in range(gy):
                    total = beside(field[z], y)
                    for other in (z - 1, z + 1):
                        if other in field:
                            total = total + field[other][y]
                    la[z, y] = field[z][y] + quarter[z, y] * total
        coef, coefs = coefs_of(fold(projs))

        projs = no_projs()
        for z in range(nz):
            scaled = []
            for y in range(gy):
                value = la[z, y]
                for other in (z - 1, z + 1):
                    if 0 <= other < nz and other // planes != z // planes:
                        value = value + quarter[z, y] * x0[other, y]
                if nz > planes:
                    la[z, y] = value
                scaled.append(value * shared(2, z, y))
            projs[z % 2] = projs[z % 2] + project(z, scaled)

        src, dst = la, lb
        for step in range(1, ITERS):
            last = step == ITERS - 1
            next_proj = fold(projs) - damp * coef
            for z in range(nz):
                values = back(coefs, z)
                for y in range(gy):
                    state[z, y] = src[z, y] - bh[z, y] * values[y]
            coef, coefs = coefs_of(next_proj)
            projs = no_projs()
            for z in range(nz):
                plane = [state[z, y] for y in range(gy)]
                scaled = []
                for y in range(gy):
                    total = beside(plane, y)
                    for other in (z - 1, z + 1):
                        if 0 <= other < nz:
                            total = total + state[other, y]
                    value = 0.5 * (plane[y] + x0[z, y]) + quarter[z, y] * total
                    if not last:
                        dst[z, y] = value
                        scaled.append(value * shared(2, z, y))
                    elif first:
                        acc[z, y] = psit[z, y] * value
                    else:
                        acc[z, y] += psit[z, y] * value
                if not last:
                    projs[z % 2] = projs[z % 2] + project(z, scaled)
            src, dst = dst, src

        for z in range(nz):
            values = back(coefs, z)
            terms = [acc[z, y] - pb[z, y] * values[y] for y in range(gy)]
            if slot > 0:
                for y in range(gy):
                    acc[z, y] = terms[y]
            else:
                p = z % planes
                part[z // planes, p * gy:(p + 1) * gy, :] = reduce_rows(terms)
                if streams and p == planes - 1 and z >= planes:
                    part_copy(z // planes - 1).start()

    if slots > 1:
        acc[...] = jnp.zeros(acc.shape, jnp.float32)
    for slot in reversed(range(slots)):
        holders = sorted({h for _, _, h, s in tasks if s == slot})
        if len(holders) == n:
            solve(slot, slots == 1)
        else:
            if slot == 0:
                part[...] = jnp.zeros(part.shape, jnp.float32)

            @pl.when(functools.reduce(jnp.logical_or, [k == h for h in holders]))
            def _(slot=slot):
                solve(slot, slot == slots - 1)

    if not streams:
        for i in range(n - 1):
            part_copy(i).start()

    for i in range(2 * tiles):
        if tasks[i][0]:
            psi_copy(i).wait_send()
        else:
            @pl.when(k != tasks[i][2])
            def _():
                psi_copy(i).wait_send()
    for j in range(n):
        if j != n // 2:
            pack_copy(j, k, sibling).wait_send()

    @pl.when(k == 1)
    def _():
        for i in range(len(prior_holders)):
            e_copy(i).wait_send()

    out[0] = part[k]
    for i in range(n - 1):
        part_copy(i).wait_send()
    for j in range(1, n):
        part_arrival(j).wait()


def shards(orbitals, energies, trial_potential, local_potential, beta, support, slot_atom, dcoef):
    n, nb = lax.axis_size("slab"), lax.axis_size("blk")
    count, planes, gy, gx = orbitals.shape
    tiles = count // ROWS
    slots = -(-2 * tiles // n)
    atoms = dcoef.shape[0]
    nz, rows = n * planes, planes * gy
    orb = orbitals.reshape(tiles, ROWS, planes, gy, gx)
    f32, bf16 = jnp.float32, jnp.bfloat16
    vmem = pl.BlockSpec(memory_space=pltpu.VMEM)
    hbm = pl.BlockSpec(memory_space=pltpu.HBM)
    dma = pltpu.SemaphoreType.DMA
    field = pltpu.VMEM((nz, gy, ROWS, gx), f32)
    parts = pl.pallas_call(
        functools.partial(kernel, (n, nb, tiles, slots, planes, gy, gx, atoms)),
        out_shape=jax.ShapeDtypeStruct((n, rows, gx), f32),
        in_specs=[hbm] * 8,
        out_specs=vmem,
        scratch_shapes=[
            pltpu.VMEM((slots, n, ROWS, planes, gy, gx), bf16),
            pltpu.VMEM(energies.shape, bf16),
            pltpu.VMEM(energies.shape, bf16),
            pltpu.SMEM(slot_atom.shape, jnp.int32),
            pltpu.VMEM(beta.shape, f32),
            pltpu.VMEM(support.shape, jnp.int32),
            pltpu.VMEM((1, atoms), f32),
            pltpu.VMEM((n, 4, planes, gy, gx), f32),
            pltpu.VMEM((n, rows, gx), f32),
            pltpu.VMEM((ROWS * rows, gx), f32),
            field, field, field, field, field, field, field, field, field, field,
            pltpu.VMEM((nz, gy, ROWS, gx), jnp.int32),
            pltpu.VMEM((nz, atoms, gy * gx), bf16),
            dma((2 * tiles,)), dma((slots, n)), dma((n + 1,)), dma((7,)),
            dma((n,)), dma((n,)), dma((n,)), dma((n,)), pltpu.SemaphoreType.REGULAR, pltpu.SemaphoreType.REGULAR,
        ],
        compiler_params=pltpu.CompilerParams(
            collective_id=0, has_side_effects=True, vmem_limit_bytes=32 << 20),
    )(*[pltpu.with_memory_space_constraint(a, pltpu.HBM) for a in (
        orb, energies, slot_atom, trial_potential, local_potential, beta, support,
        dcoef.reshape(1, atoms))])
    return jnp.sum(parts, axis=0).reshape(trial_potential.shape)


def solution(mesh):
    placed = (
        P("blk", "slab", None, None),
        P("blk"),
        P("blk", "slab", None, None),
        P("slab", None, None),
        P("slab", None),
        P("slab", None),
        P("slab"),
        P(),
    )
    return jax.shard_map(
        shards, mesh=mesh, in_specs=placed, out_specs=P("blk", "slab", None, None), check_vma=False
    )
```

```python
import functools

import jax
import jax.numpy as jnp
from jax import lax
from jax.experimental import pallas as pl
from jax.experimental.pallas import tpu as pltpu
from jax.sharding import PartitionSpec as P

ITERS = 3
ROWS = 8
MESH = pl.DeviceIdType.MESH


def nt_dot(a, b):
    return lax.dot_general(a, b, (((1,), (1,)), ((), ())), preferred_element_type=jnp.float32)


def pick_lanes(values, lanes):
    return lax.gather(
        values, lanes[..., None],
        lax.GatherDimensionNumbers(
            offset_dims=(), collapsed_slice_dims=(1,), start_index_map=(1,),
            operand_batching_dims=(0,), start_indices_batching_dims=(0,)),
        slice_sizes=(1, 1), mode=lax.GatherScatterMode.PROMISE_IN_BOUNDS)


def plan(n, tiles):
    order = [0, n - 1, 1] + list(range(2, n - 1))
    held = [0] * n
    tasks = []
    for i in range(2 * tiles):
        holder = order[i] if i < n else 1 - (i - n) % 2
        tasks.append((i < tiles, i % tiles, holder, held[holder]))
        held[holder] += 1
    return tasks


def lookup(k, table):
    value = jnp.int32(0)
    for i, entry in enumerate(table):
        if entry:
            value = value + jnp.where(k == i, jnp.int32(entry), jnp.int32(0))
    return value


def kernel(
    cfg, orb, eng, slot_atom_in, pot, locp, beta_in, support_in, dcoef_in, out,
    psi_buf, e_own, e_prior, slot_atom, beta, support, dcoef, pack_buf, part,
    psi32, psit, x0, gain, quarter, bh, la, lb, state, acc, pb, ids, onehot, shift,
    psi_send, psi_recv, e_sems, in_sems, pack_send, pack_recv, part_send, part_recv, go, word,
):
    n, nb, tiles, slots, planes, gy, gx, atoms = cfg
    rows = planes * gy
    nz = n * planes
    d, k = lax.axis_index("blk"), lax.axis_index("slab")
    before = lax.rem(d + nb - 1, nb)
    after = lax.rem(d + 1, nb)
    sibling = k + 1 - 2 * lax.rem(k, 2)
    tasks = plan(n, tiles)
    root, second = n - 1, n - 2
    first_turn = sorted(range(tiles), key=lambda i: tasks[i][2] != root)
    wraps = d == nb - 1
    prior_holders = sorted({h for prior, _, h, _ in tasks if prior})
    takes_prior = functools.reduce(jnp.logical_or, [k == h for h in prior_holders])

    loads = [
        pltpu.make_async_copy(src, dst, in_sems.at[i]) for i, (src, dst) in enumerate((
            (support_in, support), (beta_in, beta), (slot_atom_in, slot_atom),
            (dcoef_in, dcoef), (pot.at[0], pack_buf.at[k, 0]), (locp, pack_buf.at[k, 1]),
            (eng, e_own)))]
    for load in loads:
        load.start()
    barrier = pltpu.get_barrier_semaphore()

    @pl.when(takes_prior)
    def _():
        for j in range(n - 1):
            pl.semaphore_signal(barrier, inc=1, device_id=(before, j), device_id_type=MESH)

    @pl.when(jnp.logical_and(takes_prior, d == 0))
    def _():
        pl.semaphore_signal(barrier, inc=1, device_id=(before, root), device_id_type=MESH)

    @pl.when(k != root)
    def _():
        pl.semaphore_signal(barrier, inc=1, device_id=(d, root), device_id_type=MESH)
        pl.semaphore_wait(barrier, len(prior_holders))

    @pl.when(k == root)
    def _():
        pl.semaphore_wait(barrier, jnp.where(wraps, n - 1 + len(prior_holders), n - 1))
        for j in reversed(range(n - 1)):
            pl.semaphore_signal(go, inc=1, device_id=(d, j), device_id_type=MESH)

    def psi_copy(i):
        prior, tile, holder, slot = tasks[i]
        return pltpu.make_async_remote_copy(
            src_ref=orb.at[tile], dst_ref=psi_buf.at[slot, k],
            send_sem=psi_send.at[i], recv_sem=psi_recv.at[slot, k],
            device_id=(after if prior else d, holder), device_id_type=MESH)

    def psi_arrival(slot, j):
        return pltpu.make_async_copy(
            psi_buf.at[slot, j], psi_buf.at[slot, j], psi_recv.at[slot, j])

    def e_copy(i):
        return pltpu.make_async_remote_copy(
            src_ref=eng, dst_ref=e_prior, send_sem=e_sems.at[i],
            recv_sem=e_sems.at[n], device_id=(after, prior_holders[i]), device_id_type=MESH)

    def pack_copy(j, slab, to):
        return pltpu.make_async_remote_copy(
            src_ref=pack_buf.at[slab], dst_ref=pack_buf.at[slab],
            send_sem=pack_send.at[j], recv_sem=pack_recv.at[slab],
            device_id=(d, to), device_id_type=MESH)

    def pack_arrival(slab):
        return pltpu.make_async_copy(
            pack_buf.at[slab], pack_buf.at[slab], pack_recv.at[slab])

    def part_copy(i):
        to = i + jnp.where(k <= i, 1, 0)
        j = lax.rem(to - k + n, n)
        return pltpu.make_async_remote_copy(
            src_ref=part.at[to], dst_ref=out.at[j],
            send_sem=part_send.at[i], recv_sem=part_recv.at[j],
            device_id=(d, to), device_id_type=MESH)

    def part_arrival(j):
        return pltpu.make_async_copy(part.at[j], out.at[j], part_recv.at[j])

    @pl.when(k == 1)
    def _():
        for i in range(len(prior_holders)):
            e_copy(i).start()

    @pl.when(jnp.logical_and(wraps, k < n // 2))
    def _():
        for i in first_turn:
            psi_copy(i).start()

    @pl.when(jnp.logical_and(wraps, k >= n // 2))
    def _():
        for i in range(tiles):
            psi_copy(i).start()

    @pl.when(k == second)
    def _():
        pl.semaphore_wait(go, 1)

    @pl.when(jnp.logical_and(k == second, jnp.logical_not(wraps)))
    def _():
        pl.semaphore_signal(word, inc=1, device_id=(d, root), device_id_type=MESH)

    for load in loads:
        load.wait()

    sub_rows = lax.broadcasted_iota(jnp.int32, (rows, gx), 0)
    sub_cols = lax.broadcasted_iota(jnp.int32, (gx, gx), 0)
    lefts, rights = [], []
    for s in range(beta.shape[0]):
        cell = support[s:s + 1, :]
        value = beta[s:s + 1, :]
        b1 = value.astype(jnp.bfloat16).astype(jnp.float32)
        b2 = (value - b1).astype(jnp.bfloat16).astype(jnp.float32)
        b3 = value - b1 - b2
        hit = sub_rows == lax.shift_right_logical(cell, 7)
        atom = jnp.full((1, 1), slot_atom[s], jnp.int32).astype(jnp.float32)
        lefts.append(jnp.concatenate(
            [jnp.where(hit, b1, 0.0), jnp.where(hit, b2, 0.0),
             jnp.where(hit, b3, 0.0), jnp.where(hit, atom, 0.0)], axis=0).astype(jnp.bfloat16))
        rights.append(jnp.where(sub_cols == (cell & 127), 1.0, 0.0).astype(jnp.bfloat16))
    cells = nt_dot(jnp.concatenate(lefts, axis=1), jnp.concatenate(rights, axis=1))
    cellwise = cells[:rows] + cells[rows:2 * rows] + cells[2 * rows:3 * rows]
    pack_buf[k, 2] = cellwise.reshape(planes, gy, gx)
    pack_buf[k, 3] = cells[3 * rows:].reshape(planes, gy, gx)

    @pl.when(k < second)
    def _():
        pl.semaphore_wait(go, 1)

    pack_copy(0, k, sibling).start()
    for j in range(1, n // 2):
        pack_copy(j, k, lax.rem(k + 2 * j, n)).start()
    for i in range(tiles, 2 * tiles):
        _, tile, holder, slot = tasks[i]

        @pl.when(k == holder)
        def _():
            pltpu.make_async_copy(
                orb.at[tile], psi_buf.at[slot, k], psi_recv.at[slot, k]).start()

        @pl.when(k != holder)
        def _():
            psi_copy(i).start()

    @pl.when(jnp.logical_and(k == root, jnp.logical_not(wraps)))
    def _():
        pl.semaphore_wait(word, 1)

    @pl.when(jnp.logical_not(wraps))
    def _():
        for i in range(tiles):
            psi_copy(i).start()

    strength = dcoef[...]
    atom_ids = lax.broadcasted_iota(jnp.int32, (atoms, gx), 0).astype(jnp.float32)
    for j in range(1, n // 2):
        slab = lax.rem(k + 2 * j, n)
        pack_arrival(slab).wait()
        pack_copy(n // 2 + j, slab, sibling).start()
    for j in range(n // 2):
        pack_arrival(lax.rem(sibling + 2 * j, n)).wait()

    for z in range(nz):
        slab, p = z // planes, z % planes
        for y in range(gy):
            at = pack_buf[slab, 3, p, y:y + 1, :]
            onehot[z, :, y * gx:(y + 1) * gx] = jnp.where(atom_ids == at, 1.0, 0.0).astype(jnp.bfloat16)
            ids[z, y] = jnp.broadcast_to(at, (ROWS, gx)).astype(jnp.int32)

    apart = (lax.broadcasted_iota(jnp.int32, (2 * gx, gx), 0)
             - lax.broadcasted_iota(jnp.int32, (2 * gx, gx), 1)) & (gx - 1)
    shift[...] = jnp.where((apart == 1) | (apart == gx - 1), 1.0, 0.0).astype(jnp.bfloat16)

    def add_along_x(plane, ys):
        whole = jnp.concatenate([plane[y] for y in ys], axis=0)
        high = whole.astype(jnp.bfloat16)
        low = (whole - high.astype(jnp.float32)).astype(jnp.bfloat16)
        sums = jnp.dot(jnp.concatenate([high, low], axis=1), shift[...],
                       preferred_element_type=jnp.float32)
        return {y: sums[i * ROWS:(i + 1) * ROWS] for i, y in enumerate(ys)}

    def shared(which, z, y):
        return pack_buf[z // planes, which, z % planes, y:y + 1, :]

    def split(value):
        high = value.astype(jnp.bfloat16).astype(jnp.float32)
        return high, value - high

    def project(z, tiles_of_plane):
        both = jnp.concatenate(
            [jnp.concatenate(split(t), axis=0).astype(jnp.bfloat16) for t in tiles_of_plane], axis=1)
        return nt_dot(both, onehot[z])

    def fold(projs):
        total = projs[0] * strength + projs[1] * strength
        return total[:ROWS] + total[ROWS:]

    def no_projs():
        return [jnp.zeros((2 * ROWS, atoms), jnp.float32) for _ in range(2)]

    def coefs_of(coefs):
        if atoms == gx:
            return coefs, coefs
        return coefs, jnp.concatenate([coefs, jnp.zeros((ROWS, gx - atoms), jnp.float32)], axis=1)

    def back(coefs, z):
        return [pick_lanes(coefs, ids[z, y]) for y in range(gy)]

    def beside(plane, y):
        return (plane[(y + 1) % gy] + plane[(y - 1) % gy]
                + pltpu.roll(plane[y], 1, 1) + pltpu.roll(plane[y], gx - 1, 1))

    sub = lax.broadcasted_iota(jnp.int32, (ROWS, gx), 0)

    def reduce_rows(values):
        shift = 1
        while len(values) > 1:
            odd = (sub & shift) != 0
            merged = []
            for a, b in zip(values[0::2], values[1::2]):
                merged.append(jnp.where(odd, b, a) + pltpu.roll(jnp.where(odd, a, b), shift, 0))
            values, shift = merged, 2 * shift
        return values[0]

    arrival_order = [j + 1 - 2 * (j % 2) for j in range(n)]

    streams = len({h for _, _, h, s in tasks if s == 0}) == n

    def solve(slot, first):
        held_by = [(prior, tile, h) for prior, tile, h, s in tasks if s == slot]
        tile_of = lookup(k, [next((t for _, t, h in held_by if h == i), 0) for i in range(n)])
        priors = [h for prior, _, h in held_by if prior]
        if not priors:
            held = e_own[...].astype(jnp.float32)
        else:
            is_prior = functools.reduce(jnp.logical_or, [k == h for h in priors])

            @pl.when(is_prior)
            def _():
                e_copy(0).wait_recv()

            @pl.when(jnp.logical_not(is_prior))
            def _():
                e_prior[...] = e_own[...]

            held = e_prior[...].astype(jnp.float32)
        held = held.reshape(1, tiles * ROWS)
        wanted = lax.broadcasted_iota(jnp.int32, (ROWS, tiles * ROWS), 0) + ROWS * tile_of
        mine = wanted == lax.broadcasted_iota(jnp.int32, (ROWS, tiles * ROWS), 1)
        energy = jnp.broadcast_to(
            jnp.sum(jnp.where(mine, held, 0.0), axis=1, keepdims=True), (ROWS, gx))

        damps = no_projs()
        for z in range(nz):
            scaled = []
            for y in range(gy):
                inv = 1.0 / (3.0 + shared(1, z, y) - energy)
                bv = shared(2, z, y)
                half_inv = 0.5 * bv * inv
                gain[z, y] = -(shared(0, z, y) * inv)
                quarter[z, y] = 0.25 * inv
                bh[z, y] = half_inv
                scaled.append(bv * half_inv)
            damps[z % 2] = damps[z % 2] + project(z, scaled)
        damp = fold(damps)

        projs = no_projs()
        for j in arrival_order:
            psi_arrival(slot, j).wait()
            psi32[...] = psi_buf[slot, j].astype(jnp.float32).reshape(ROWS * rows, gx)
            zs = range(j * planes, (j + 1) * planes)
            field = {}
            for z in zs:
                scaled, field[z] = [], []
                for y in range(gy):
                    psi = psi32[pl.ds(z % planes * gy + y, ROWS, stride=rows), :]
                    start = gain[z, y] * psi
                    psit[z, y] = psi
                    pb[z, y] = psi * bh[z, y]
                    x0[z, y] = start
                    field[z].append(start)
                    scaled.append(start * shared(2, z, y))
                projs[z % 2] = projs[z % 2] + project(z, scaled)
            for z in zs:
                for y in range(gy):
                    total = beside(field[z], y)
                    for other in (z - 1, z + 1):
                        if other in field:
                            total = total + field[other][y]
                    la[z, y] = field[z][y] + quarter[z, y] * total
        coef, coefs = coefs_of(fold(projs))

        projs = no_projs()
        for z in range(nz):
            scaled = []
            for y in range(gy):
                value = la[z, y]
                for other in (z - 1, z + 1):
                    if 0 <= other < nz and other // planes != z // planes:
                        value = value + quarter[z, y] * x0[other, y]
                if nz > planes:
                    la[z, y] = value
                scaled.append(value * shared(2, z, y))
            projs[z % 2] = projs[z % 2] + project(z, scaled)

        src, dst = la, lb
        for step in range(1, ITERS):
            last = step == ITERS - 1
            next_proj = fold(projs) - damp * coef
            for z in range(nz):
                values = back(coefs, z)
                for y in range(gy):
                    state[z, y] = src[z, y] - bh[z, y] * values[y]
            coef, coefs = coefs_of(next_proj)
            projs = no_projs()
            for z in range(nz):
                plane = [state[z, y] for y in range(gy)]
                scaled = []
                added = add_along_x(plane, range(gy)) if last else {}
                for y in range(gy):
                    if y in added:
                        total = plane[(y + 1) % gy] + plane[(y - 1) % gy] + added[y]
                    else:
                        total = beside(plane, y)
                    for other in (z - 1, z + 1):
                        if 0 <= other < nz:
                            total = total + state[other, y]
                    value = 0.5 * (plane[y] + x0[z, y]) + quarter[z, y] * total
                    if not last:
                        dst[z, y] = value
                        scaled.append(value * shared(2, z, y))
                    elif first:
                        acc[z, y] = psit[z, y] * value
                    else:
                        acc[z, y] += psit[z, y] * value
                if not last:
                    projs[z % 2] = projs[z % 2] + project(z, scaled)
            src, dst = dst, src

        for z in range(nz):
            values = back(coefs, z)
            terms = [acc[z, y] - pb[z, y] * values[y] for y in range(gy)]
            if slot > 0:
                for y in range(gy):
                    acc[z, y] = terms[y]
            else:
                p = z % planes
                part[z // planes, p * gy:(p + 1) * gy, :] = reduce_rows(terms)
                if streams and z == 2 * planes - 1:
                    part_copy(0).start()

    if slots > 1:
        acc[...] = jnp.zeros(acc.shape, jnp.float32)
    for slot in reversed(range(slots)):
        holders = sorted({h for _, _, h, s in tasks if s == slot})
        if len(holders) == n:
            solve(slot, slots == 1)
        else:
            if slot == 0:
                part[...] = jnp.zeros(part.shape, jnp.float32)

            @pl.when(functools.reduce(jnp.logical_or, [k == h for h in holders]))
            def _(slot=slot):
                solve(slot, slot == slots - 1)

    for i in range(1 if streams else 0, n - 1):
        part_copy(i).start()

    for i in range(2 * tiles):
        if tasks[i][0]:
            psi_copy(i).wait_send()
        else:
            @pl.when(k != tasks[i][2])
            def _():
                psi_copy(i).wait_send()
    for j in range(n):
        if j != n // 2:
            pack_copy(j, k, sibling).wait_send()

    @pl.when(k == 1)
    def _():
        for i in range(len(prior_holders)):
            e_copy(i).wait_send()

    out[0] = part[k]
    for i in range(n - 1):
        part_copy(i).wait_send()
    for j in range(1, n):
        part_arrival(j).wait()


def shards(orbitals, energies, trial_potential, local_potential, beta, support, slot_atom, dcoef):
    n, nb = lax.axis_size("slab"), lax.axis_size("blk")
    count, planes, gy, gx = orbitals.shape
    tiles = count // ROWS
    slots = -(-2 * tiles // n)
    atoms = dcoef.shape[0]
    nz, rows = n * planes, planes * gy
    orb = orbitals.reshape(tiles, ROWS, planes, gy, gx)
    f32, bf16 = jnp.float32, jnp.bfloat16
    vmem = pl.BlockSpec(memory_space=pltpu.VMEM)
    hbm = pl.BlockSpec(memory_space=pltpu.HBM)
    dma = pltpu.SemaphoreType.DMA
    field = pltpu.VMEM((nz, gy, ROWS, gx), f32)
    parts = pl.pallas_call(
        functools.partial(kernel, (n, nb, tiles, slots, planes, gy, gx, atoms)),
        out_shape=jax.ShapeDtypeStruct((n, rows, gx), f32),
        in_specs=[hbm] * 8,
        out_specs=vmem,
        scratch_shapes=[
            pltpu.VMEM((slots, n, ROWS, planes, gy, gx), bf16),
            pltpu.VMEM(energies.shape, bf16),
            pltpu.VMEM(energies.shape, bf16),
            pltpu.SMEM(slot_atom.shape, jnp.int32),
            pltpu.VMEM(beta.shape, f32),
            pltpu.VMEM(support.shape, jnp.int32),
            pltpu.VMEM((1, atoms), f32),
            pltpu.VMEM((n, 4, planes, gy, gx), f32),
            pltpu.VMEM((n, rows, gx), f32),
            pltpu.VMEM((ROWS * rows, gx), f32),
            field, field, field, field, field, field, field, field, field, field,
            pltpu.VMEM((nz, gy, ROWS, gx), jnp.int32),
            pltpu.VMEM((nz, atoms, gy * gx), bf16),
            pltpu.VMEM((2 * gx, gx), bf16),
            dma((2 * tiles,)), dma((slots, n)), dma((n + 1,)), dma((7,)),
            dma((n,)), dma((n,)), dma((n,)), dma((n,)), pltpu.SemaphoreType.REGULAR, pltpu.SemaphoreType.REGULAR,
        ],
        compiler_params=pltpu.CompilerParams(
            collective_id=0, has_side_effects=True, vmem_limit_bytes=32 << 20),
    )(*[pltpu.with_memory_space_constraint(a, pltpu.HBM) for a in (
        orb, energies, slot_atom, trial_potential, local_potential, beta, support,
        dcoef.reshape(1, atoms))])
    return jnp.sum(parts, axis=0).reshape(trial_potential.shape)


def solution(mesh):
    placed = (
        P("blk", "slab", None, None),
        P("blk"),
        P("blk", "slab", None, None),
        P("slab", None, None),
        P("slab", None),
        P("slab", None),
        P("slab"),
        P(),
    )
    return jax.shard_map(
        shards, mesh=mesh, in_specs=placed, out_specs=P("blk", "slab", None, None), check_vma=False
    )
```

```python
import functools

import jax
import jax.numpy as jnp
from jax import lax
from jax.experimental import pallas as pl
from jax.experimental.pallas import tpu as pltpu
from jax.sharding import PartitionSpec as P

ITERS = 3
ROWS = 8
MESH = pl.DeviceIdType.MESH


def nt_dot(a, b):
    return lax.dot_general(a, b, (((1,), (1,)), ((), ())), preferred_element_type=jnp.float32)


def pick_lanes(values, lanes):
    return lax.gather(
        values, lanes[..., None],
        lax.GatherDimensionNumbers(
            offset_dims=(), collapsed_slice_dims=(1,), start_index_map=(1,),
            operand_batching_dims=(0,), start_indices_batching_dims=(0,)),
        slice_sizes=(1, 1), mode=lax.GatherScatterMode.PROMISE_IN_BOUNDS)


def plan(n, tiles):
    order = [0, n - 1, 1] + list(range(2, n - 1))
    held = [0] * n
    tasks = []
    for i in range(2 * tiles):
        holder = order[i] if i < n else 1 - (i - n) % 2
        tasks.append((i < tiles, i % tiles, holder, held[holder]))
        held[holder] += 1
    return tasks


def lookup(k, table):
    value = jnp.int32(0)
    for i, entry in enumerate(table):
        if entry:
            value = value + jnp.where(k == i, jnp.int32(entry), jnp.int32(0))
    return value


def kernel(
    cfg, orb, eng, slot_atom_in, pot, locp, beta_in, support_in, dcoef_in, out,
    psi_buf, e_own, e_prior, slot_atom, beta, support, dcoef, pack_buf, part,
    psi32, psit, x0, gain, quarter, bh, la, lb, state, acc, pb, ids, onehot, shift,
    psi_send, psi_recv, e_sems, in_sems, pack_send, pack_recv, part_send, part_recv, go, word,
):
    n, nb, tiles, slots, planes, gy, gx, atoms = cfg
    rows = planes * gy
    nz = n * planes
    d, k = lax.axis_index("blk"), lax.axis_index("slab")
    before = lax.rem(d + nb - 1, nb)
    after = lax.rem(d + 1, nb)
    sibling = k + 1 - 2 * lax.rem(k, 2)
    tasks = plan(n, tiles)
    root, second = n - 1, n - 2
    first_turn = sorted(range(tiles), key=lambda i: tasks[i][2] != root)
    wraps = d == nb - 1
    prior_holders = sorted({h for prior, _, h, _ in tasks if prior})
    takes_prior = functools.reduce(jnp.logical_or, [k == h for h in prior_holders])

    loads = [
        pltpu.make_async_copy(src, dst, in_sems.at[i]) for i, (src, dst) in enumerate((
            (support_in, support), (beta_in, beta), (slot_atom_in, slot_atom),
            (dcoef_in, dcoef), (pot.at[0], pack_buf.at[k, 0]), (locp, pack_buf.at[k, 1]),
            (eng, e_own)))]
    for load in loads:
        load.start()
    barrier = pltpu.get_barrier_semaphore()

    @pl.when(takes_prior)
    def _():
        for j in range(n - 1):
            pl.semaphore_signal(barrier, inc=1, device_id=(before, j), device_id_type=MESH)

    @pl.when(jnp.logical_and(takes_prior, d == 0))
    def _():
        pl.semaphore_signal(barrier, inc=1, device_id=(before, root), device_id_type=MESH)

    @pl.when(k != root)
    def _():
        pl.semaphore_signal(barrier, inc=1, device_id=(d, root), device_id_type=MESH)
        pl.semaphore_wait(barrier, len(prior_holders))

    @pl.when(k == root)
    def _():
        pl.semaphore_wait(barrier, jnp.where(wraps, n - 1 + len(prior_holders), n - 1))
        for j in reversed(range(n - 1)):
            pl.semaphore_signal(go, inc=1, device_id=(d, j), device_id_type=MESH)

    def psi_copy(i):
        prior, tile, holder, slot = tasks[i]
        return pltpu.make_async_remote_copy(
            src_ref=orb.at[tile], dst_ref=psi_buf.at[slot, k],
            send_sem=psi_send.at[i], recv_sem=psi_recv.at[slot, k],
            device_id=(after if prior else d, holder), device_id_type=MESH)

    def psi_arrival(slot, j):
        return pltpu.make_async_copy(
            psi_buf.at[slot, j], psi_buf.at[slot, j], psi_recv.at[slot, j])

    def e_copy(i):
        return pltpu.make_async_remote_copy(
            src_ref=eng, dst_ref=e_prior, send_sem=e_sems.at[i],
            recv_sem=e_sems.at[n], device_id=(after, prior_holders[i]), device_id_type=MESH)

    def pack_copy(j, slab, to):
        return pltpu.make_async_remote_copy(
            src_ref=pack_buf.at[slab], dst_ref=pack_buf.at[slab],
            send_sem=pack_send.at[j], recv_sem=pack_recv.at[slab],
            device_id=(d, to), device_id_type=MESH)

    def pack_arrival(slab):
        return pltpu.make_async_copy(
            pack_buf.at[slab], pack_buf.at[slab], pack_recv.at[slab])

    def part_copy(i):
        to = i + jnp.where(k <= i, 1, 0)
        j = lax.rem(to - k + n, n)
        return pltpu.make_async_remote_copy(
            src_ref=part.at[to], dst_ref=out.at[j],
            send_sem=part_send.at[i], recv_sem=part_recv.at[j],
            device_id=(d, to), device_id_type=MESH)

    def part_arrival(j):
        return pltpu.make_async_copy(part.at[j], out.at[j], part_recv.at[j])

    @pl.when(k == 1)
    def _():
        for i in range(len(prior_holders)):
            e_copy(i).start()

    def far_copies(here, order):
        @pl.when(jnp.logical_and(wraps, here))
        def _():
            for i in order:
                psi_copy(i).start()

    far_copies(jnp.logical_or(k == 0, k == root), first_turn)
    far_copies(k == 1, [tiles - 1] + list(range(tiles - 1)))
    far_copies(jnp.logical_and(k > 1, k != root), range(tiles))

    @pl.when(k == second)
    def _():
        pl.semaphore_wait(go, 1)

    @pl.when(jnp.logical_and(k == second, jnp.logical_not(wraps)))
    def _():
        pl.semaphore_signal(word, inc=1, device_id=(d, root), device_id_type=MESH)

    for load in loads:
        load.wait()

    sub_rows = lax.broadcasted_iota(jnp.int32, (rows, gx), 0)
    sub_cols = lax.broadcasted_iota(jnp.int32, (gx, gx), 0)
    lefts, rights = [], []
    for s in range(beta.shape[0]):
        cell = support[s:s + 1, :]
        value = beta[s:s + 1, :]
        b1 = value.astype(jnp.bfloat16).astype(jnp.float32)
        b2 = (value - b1).astype(jnp.bfloat16).astype(jnp.float32)
        b3 = value - b1 - b2
        hit = sub_rows == lax.shift_right_logical(cell, 7)
        atom = jnp.full((1, 1), slot_atom[s], jnp.int32).astype(jnp.float32)
        lefts.append(jnp.concatenate(
            [jnp.where(hit, b1, 0.0), jnp.where(hit, b2, 0.0),
             jnp.where(hit, b3, 0.0), jnp.where(hit, atom, 0.0)], axis=0).astype(jnp.bfloat16))
        rights.append(jnp.where(sub_cols == (cell & 127), 1.0, 0.0).astype(jnp.bfloat16))
    cells = nt_dot(jnp.concatenate(lefts, axis=1), jnp.concatenate(rights, axis=1))
    cellwise = cells[:rows] + cells[rows:2 * rows] + cells[2 * rows:3 * rows]
    pack_buf[k, 2] = cellwise.reshape(planes, gy, gx)
    pack_buf[k, 3] = cells[3 * rows:].reshape(planes, gy, gx)

    @pl.when(k < second)
    def _():
        pl.semaphore_wait(go, 1)

    pack_copy(0, k, sibling).start()
    for j in range(1, n // 2):
        pack_copy(j, k, lax.rem(k + 2 * j, n)).start()
    for i in range(tiles, 2 * tiles):
        _, tile, holder, slot = tasks[i]

        @pl.when(k == holder)
        def _():
            pltpu.make_async_copy(
                orb.at[tile], psi_buf.at[slot, k], psi_recv.at[slot, k]).start()

        @pl.when(k != holder)
        def _():
            psi_copy(i).start()

    @pl.when(jnp.logical_and(k == root, jnp.logical_not(wraps)))
    def _():
        pl.semaphore_wait(word, 1)

    @pl.when(jnp.logical_not(wraps))
    def _():
        for i in range(tiles):
            psi_copy(i).start()

    strength = dcoef[...]
    atom_ids = lax.broadcasted_iota(jnp.int32, (atoms, gx), 0).astype(jnp.float32)
    for j in range(1, n // 2):
        slab = lax.rem(k + 2 * j, n)
        pack_arrival(slab).wait()
        pack_copy(n // 2 + j, slab, sibling).start()
    for j in range(n // 2):
        pack_arrival(lax.rem(sibling + 2 * j, n)).wait()

    for z in range(nz):
        slab, p = z // planes, z % planes
        for y in range(gy):
            at = pack_buf[slab, 3, p, y:y + 1, :]
            onehot[z, :, y * gx:(y + 1) * gx] = jnp.where(atom_ids == at, 1.0, 0.0).astype(jnp.bfloat16)
            ids[z, y] = jnp.broadcast_to(at, (ROWS, gx)).astype(jnp.int32)

    apart = (lax.broadcasted_iota(jnp.int32, (2 * gx, gx), 0)
             - lax.broadcasted_iota(jnp.int32, (2 * gx, gx), 1)) & (gx - 1)
    shift[...] = jnp.where((apart == 1) | (apart == gx - 1), 1.0, 0.0).astype(jnp.bfloat16)

    def add_along_x(plane, ys):
        whole = jnp.concatenate([plane[y] for y in ys], axis=0)
        high = whole.astype(jnp.bfloat16)
        low = (whole - high.astype(jnp.float32)).astype(jnp.bfloat16)
        sums = jnp.dot(jnp.concatenate([high, low], axis=1), shift[...],
                       preferred_element_type=jnp.float32)
        return {y: sums[i * ROWS:(i + 1) * ROWS] for i, y in enumerate(ys)}

    def shared(which, z, y):
        return pack_buf[z // planes, which, z % planes, y:y + 1, :]

    def split(value):
        high = value.astype(jnp.bfloat16).astype(jnp.float32)
        return high, value - high

    def project(z, tiles_of_plane):
        both = jnp.concatenate(
            [jnp.concatenate(split(t), axis=0).astype(jnp.bfloat16) for t in tiles_of_plane], axis=1)
        return nt_dot(both, onehot[z])

    def fold(projs):
        total = projs[0] * strength + projs[1] * strength
        return total[:ROWS] + total[ROWS:]

    def no_projs():
        return [jnp.zeros((2 * ROWS, atoms), jnp.float32) for _ in range(2)]

    def coefs_of(coefs):
        if atoms == gx:
            return coefs, coefs
        return coefs, jnp.concatenate([coefs, jnp.zeros((ROWS, gx - atoms), jnp.float32)], axis=1)

    def back(coefs, z):
        return [pick_lanes(coefs, ids[z, y]) for y in range(gy)]

    def beside(plane, y):
        return (plane[(y + 1) % gy] + plane[(y - 1) % gy]
                + pltpu.roll(plane[y], 1, 1) + pltpu.roll(plane[y], gx - 1, 1))

    sub = lax.broadcasted_iota(jnp.int32, (ROWS, gx), 0)

    def reduce_rows(values):
        shift = 1
        while len(values) > 1:
            odd = (sub & shift) != 0
            merged = []
            for a, b in zip(values[0::2], values[1::2]):
                merged.append(jnp.where(odd, b, a) + pltpu.roll(jnp.where(odd, a, b), shift, 0))
            values, shift = merged, 2 * shift
        return values[0]

    arrival_order = [j + 1 - 2 * (j % 2) for j in range(n)]

    streams = len({h for _, _, h, s in tasks if s == 0}) == n

    def solve(slot, first):
        held_by = [(prior, tile, h) for prior, tile, h, s in tasks if s == slot]
        tile_of = lookup(k, [next((t for _, t, h in held_by if h == i), 0) for i in range(n)])
        priors = [h for prior, _, h in held_by if prior]
        if not priors:
            held = e_own[...].astype(jnp.float32)
        else:
            is_prior = functools.reduce(jnp.logical_or, [k == h for h in priors])

            @pl.when(is_prior)
            def _():
                e_copy(0).wait_recv()

            @pl.when(jnp.logical_not(is_prior))
            def _():
                e_prior[...] = e_own[...]

            held = e_prior[...].astype(jnp.float32)
        held = held.reshape(1, tiles * ROWS)
        wanted = lax.broadcasted_iota(jnp.int32, (ROWS, tiles * ROWS), 0) + ROWS * tile_of
        mine = wanted == lax.broadcasted_iota(jnp.int32, (ROWS, tiles * ROWS), 1)
        energy = jnp.broadcast_to(
            jnp.sum(jnp.where(mine, held, 0.0), axis=1, keepdims=True), (ROWS, gx))

        damps = no_projs()
        for z in range(nz):
            scaled = []
            for y in range(gy):
                inv = 1.0 / (3.0 + shared(1, z, y) - energy)
                bv = shared(2, z, y)
                half_inv = 0.5 * bv * inv
                gain[z, y] = -(shared(0, z, y) * inv)
                quarter[z, y] = 0.25 * inv
                bh[z, y] = half_inv
                scaled.append(bv * half_inv)
            damps[z % 2] = damps[z % 2] + project(z, scaled)
        damp = fold(damps)

        projs = no_projs()
        for j in arrival_order:
            psi_arrival(slot, j).wait()
            psi32[...] = psi_buf[slot, j].astype(jnp.float32).reshape(ROWS * rows, gx)
            zs = range(j * planes, (j + 1) * planes)
            field = {}
            for z in zs:
                scaled, field[z] = [], []
                for y in range(gy):
                    psi = psi32[pl.ds(z % planes * gy + y, ROWS, stride=rows), :]
                    start = gain[z, y] * psi
                    psit[z, y] = psi
                    pb[z, y] = psi * bh[z, y]
                    x0[z, y] = start
                    field[z].append(start)
                    scaled.append(start * shared(2, z, y))
                projs[z % 2] = projs[z % 2] + project(z, scaled)
            for z in zs:
                for y in range(gy):
                    total = beside(field[z], y)
                    for other in (z - 1, z + 1):
                        if other in field:
                            total = total + field[other][y]
                    la[z, y] = field[z][y] + quarter[z, y] * total
        coef, coefs = coefs_of(fold(projs))

        projs = no_projs()
        for z in range(nz):
            scaled = []
            for y in range(gy):
                value = la[z, y]
                for other in (z - 1, z + 1):
                    if 0 <= other < nz and other // planes != z // planes:
                        value = value + quarter[z, y] * x0[other, y]
                if nz > planes:
                    la[z, y] = value
                scaled.append(value * shared(2, z, y))
            projs[z % 2] = projs[z % 2] + project(z, scaled)

        src, dst = la, lb
        for step in range(1, ITERS):
            last = step == ITERS - 1
            next_proj = fold(projs) - damp * coef
            for z in range(nz):
                values = back(coefs, z)
                for y in range(gy):
                    state[z, y] = src[z, y] - bh[z, y] * values[y]
            coef, coefs = coefs_of(next_proj)
            projs = no_projs()
            for z in range(nz):
                plane = [state[z, y] for y in range(gy)]
                scaled = []
                added = add_along_x(plane, range(gy)) if last else {}
                for y in range(gy):
                    if y in added:
                        total = plane[(y + 1) % gy] + plane[(y - 1) % gy] + added[y]
                    else:
                        total = beside(plane, y)
                    for other in (z - 1, z + 1):
                        if 0 <= other < nz:
                            total = total + state[other, y]
                    value = 0.5 * (plane[y] + x0[z, y]) + quarter[z, y] * total
                    if not last:
                        dst[z, y] = value
                        scaled.append(value * shared(2, z, y))
                    elif first:
                        acc[z, y] = psit[z, y] * value
                    else:
                        acc[z, y] += psit[z, y] * value
                if not last:
                    projs[z % 2] = projs[z % 2] + project(z, scaled)
            src, dst = dst, src

        for z in range(nz):
            values = back(coefs, z)
            terms = [acc[z, y] - pb[z, y] * values[y] for y in range(gy)]
            if slot > 0:
                for y in range(gy):
                    acc[z, y] = terms[y]
            else:
                p = z % planes
                part[z // planes, p * gy:(p + 1) * gy, :] = reduce_rows(terms)
                if streams and z == 2 * planes - 1:
                    part_copy(0).start()

    if slots > 1:
        acc[...] = jnp.zeros(acc.shape, jnp.float32)
    for slot in reversed(range(slots)):
        holders = sorted({h for _, _, h, s in tasks if s == slot})
        if len(holders) == n:
            solve(slot, slots == 1)
        else:
            if slot == 0:
                part[...] = jnp.zeros(part.shape, jnp.float32)

            @pl.when(functools.reduce(jnp.logical_or, [k == h for h in holders]))
            def _(slot=slot):
                solve(slot, slot == slots - 1)

    for i in range(1 if streams else 0, n - 1):
        part_copy(i).start()

    for i in range(2 * tiles):
        if tasks[i][0]:
            psi_copy(i).wait_send()
        else:
            @pl.when(k != tasks[i][2])
            def _():
                psi_copy(i).wait_send()
    for j in range(n):
        if j != n // 2:
            pack_copy(j, k, sibling).wait_send()

    @pl.when(k == 1)
    def _():
        for i in range(len(prior_holders)):
            e_copy(i).wait_send()

    out[0] = part[k]
    for i in range(n - 1):
        part_copy(i).wait_send()
    for j in range(1, n):
        part_arrival(j).wait()


def shards(orbitals, energies, trial_potential, local_potential, beta, support, slot_atom, dcoef):
    n, nb = lax.axis_size("slab"), lax.axis_size("blk")
    count, planes, gy, gx = orbitals.shape
    tiles = count // ROWS
    slots = -(-2 * tiles // n)
    atoms = dcoef.shape[0]
    nz, rows = n * planes, planes * gy
    orb = orbitals.reshape(tiles, ROWS, planes, gy, gx)
    f32, bf16 = jnp.float32, jnp.bfloat16
    vmem = pl.BlockSpec(memory_space=pltpu.VMEM)
    hbm = pl.BlockSpec(memory_space=pltpu.HBM)
    dma = pltpu.SemaphoreType.DMA
    field = pltpu.VMEM((nz, gy, ROWS, gx), f32)
    parts = pl.pallas_call(
        functools.partial(kernel, (n, nb, tiles, slots, planes, gy, gx, atoms)),
        out_shape=jax.ShapeDtypeStruct((n, rows, gx), f32),
        in_specs=[hbm] * 8,
        out_specs=vmem,
        scratch_shapes=[
            pltpu.VMEM((slots, n, ROWS, planes, gy, gx), bf16),
            pltpu.VMEM(energies.shape, bf16),
            pltpu.VMEM(energies.shape, bf16),
            pltpu.SMEM(slot_atom.shape, jnp.int32),
            pltpu.VMEM(beta.shape, f32),
            pltpu.VMEM(support.shape, jnp.int32),
            pltpu.VMEM((1, atoms), f32),
            pltpu.VMEM((n, 4, planes, gy, gx), f32),
            pltpu.VMEM((n, rows, gx), f32),
            pltpu.VMEM((ROWS * rows, gx), f32),
            field, field, field, field, field, field, field, field, field, field,
            pltpu.VMEM((nz, gy, ROWS, gx), jnp.int32),
            pltpu.VMEM((nz, atoms, gy * gx), bf16),
            pltpu.VMEM((2 * gx, gx), bf16),
            dma((2 * tiles,)), dma((slots, n)), dma((n + 1,)), dma((7,)),
            dma((n,)), dma((n,)), dma((n,)), dma((n,)), pltpu.SemaphoreType.REGULAR, pltpu.SemaphoreType.REGULAR,
        ],
        compiler_params=pltpu.CompilerParams(
            collective_id=0, has_side_effects=True, vmem_limit_bytes=32 << 20),
    )(*[pltpu.with_memory_space_constraint(a, pltpu.HBM) for a in (
        orb, energies, slot_atom, trial_potential, local_potential, beta, support,
        dcoef.reshape(1, atoms))])
    return jnp.sum(parts, axis=0).reshape(trial_potential.shape)


def solution(mesh):
    placed = (
        P("blk", "slab", None, None),
        P("blk"),
        P("blk", "slab", None, None),
        P("slab", None, None),
        P("slab", None),
        P("slab", None),
        P("slab"),
        P(),
    )
    return jax.shard_map(
        shards, mesh=mesh, in_specs=placed, out_specs=P("blk", "slab", None, None), check_vma=False
    )
```
